512 devices in a mesh: dp: 32 (over z, core), ctx: 16 (over y, x).
Axes of the slice: x: 4, y: 4, z: 16, core: 2. Of those that a mesh axis runs over, the one named last changes fastest.
Arguments:
- queries: bfloat16 [65536, 4096], P(('dp', 'ctx')), parts along dimension 0, may hold values from -9 to 9
- keys: bfloat16 [65536, 512], P(('dp', 'ctx')), parts along dimension 0, may hold values from -9 to 9
- values: bfloat16 [65536, 512], P(('dp', 'ctx')), parts along dimension 0, may hold values from -6 to 6
- grad_out: bfloat16 [65536, 4096], P(('dp', 'ctx')), parts along dimension 0, may hold values from -6 to 6
- doc_blocks: int32 [256], P('dp'), parts along dimension 0, may hold values from 1 to 9, 32 in all
Outputs:
- output: bfloat16 [65536, 4096], P(('dp', 'ctx')), parts along dimension 0
- query_grad: bfloat16 [65536, 4096], P(('dp', 'ctx')), parts along dimension 0
- key_grad: bfloat16 [65536, 512], P(('dp', 'ctx')), parts along dimension 0
- value_grad: bfloat16 [65536, 512], P(('dp', 'ctx')), parts along dimension 0
The draws below stay inside these ranges and needn't reach their ends.
There are 32 independent parts, one for each index of `dp`. The reference program is written for one: setup_inputs(seed, part) draws one part's arguments, and reference() takes and returns one part's arrays. A program takes and returns all parts, laid end to end along the dimension named above; each array names one. Nothing has to cross between parts.
Inputs may be any that keep to these rules, and one draw needn't show every extreme that they name: doc_blocks sums to 32; the longest document has exactly 9 blocks.
All inputs are finite; a program needn't handle non-finite values.
Results may differ from the reference program's by a relative error of at most 0.012.
The reference program's roundings to bfloat16 on the way (of `probs_low` and `score_low`) count: a program that leaves them out, or rounds other values in their place, can miss the bound.
Values may be sent and summed in bfloat16 or wider, within the bound.
A program may use at most 128 MiB of HBM per device.

```python
import math
import jax
import jax.numpy as jnp
import numpy as np
from jax import lax

HEADS = 32
KV_HEADS = 4
HEAD_DIM = 128
TOK_DEV = 128
STRETCH = 64
TOKENS = 2048
BLOCKS = 32
DOCS = 8
DOC_MAX = 9
N_CTX = 16


def draw_queries(key, part):
    sampled = jnp.clip(jax.random.normal(jax.random.fold_in(key, 1), (TOKENS, HEADS * HEAD_DIM), jnp.float32), -6.0, 6.0)
    return sampled.astype(jnp.bfloat16)


def draw_keys(key, part):
    sampled = jnp.clip(jax.random.normal(jax.random.fold_in(key, 2), (TOKENS, KV_HEADS * HEAD_DIM), jnp.float32), -6.0, 6.0)
    return sampled.astype(jnp.bfloat16)


def steps_of(key, shape, shards, low, high):
    factor_of, own = 1.0, jax.random.fold_in(key, 6)
    for dim, parts in shards:
        steps = jnp.exp(jax.random.uniform(jax.random.fold_in(own, dim), (parts,), jnp.float32, low / len(shards), high / len(shards)))
        factor_of = factor_of * jnp.repeat(steps, shape[dim] // parts).reshape([-1 if axis == dim else 1 for axis in range(len(shape))])
    return factor_of


def profile(number_of, total, most, slope):
    weights = [(1 << 20) // math.isqrt(grade ** slope) + 1 for grade in range(2, number_of + 1)]
    spare, counts = total - most - (number_of - 1), [1] * (number_of - 1)
    while spare > 0:
        movable = [i for i in range(number_of - 1) if counts[i] < most]
        mass, left = sum([weights[i] for i in movable]), spare
        for i in movable:
            addition = min(most - counts[i], max(1, left * weights[i] // mass), spare)
            counts[i] = counts[i] + addition
            spare = spare - addition
    return np.array([most] + counts)


def uneven(stream_key, number_of, total, bound, slope):
    if number_of == 2:
        one = jax.random.randint(stream_key, (), max(1, total - bound), min(bound, total - 1) + 1)
        return jnp.stack([one, total - one])
    sizes = jnp.asarray(profile(number_of, total, bound, slope), jnp.int32)
    couples = (number_of - 1) // 2
    donor, sink = sizes[1:1 + 2 * couples:2], sizes[2:2 + 2 * couples:2]
    margin = jnp.minimum(donor - 1, bound - sink)
    moved = jax.random.randint(jax.random.fold_in(stream_key, 1), (couples,), 0, 1 << 20) % (margin + 1)
    sizes = sizes.at[1:1 + 2 * couples:2].set(donor - moved).at[2:2 + 2 * couples:2].set(sink + moved)
    return sizes[jax.random.permutation(jax.random.fold_in(stream_key, 2), number_of)]


def noise(own_key, dims, spread, most, split=(), kind=jnp.bfloat16):
    values = jax.random.normal(own_key, dims, jnp.float32) * spread
    if len(split) > 0:
        values = steps_of(own_key, dims, split, -0.22, 0.18) * values
    return jnp.clip(values, min=-most, max=most).astype(kind)


def setup_inputs(seed: int = 0, part: int = 0) -> dict:
    streams_of = jax.random.split(jax.random.key(seed), 6)
    own_keys = jax.random.split(jax.random.fold_in(streams_of[5], part), 6)
    return {
        "queries": draw_queries(jax.random.fold_in(jax.random.fold_in(streams_of[5], part), 71), part),
        "keys": draw_keys(jax.random.fold_in(jax.random.fold_in(streams_of[5], part), 71), part),
        "values": noise(own_keys[2], (TOKENS, KV_HEADS * HEAD_DIM), 1.0, 6.0, ((0, 16),)),
        "grad_out": noise(own_keys[3], (TOKENS, HEADS * HEAD_DIM), 1.0, 6.0, ((0, 16),)),
        "doc_blocks": uneven(own_keys[4], DOCS, BLOCKS, DOC_MAX, 2).astype(jnp.int32),
    }


def reference(queries, keys, values, grad_out, doc_blocks):
    groups = HEADS // KV_HEADS
    score_scale = HEAD_DIM ** -0.5
    row_ids = jnp.arange(TOKENS, dtype=jnp.int32)
    device = row_ids // TOK_DEV
    second = (row_ids % TOK_DEV) // STRETCH
    block_of = jnp.where(second == 0, device, BLOCKS - 1 - device)
    position = block_of * STRETCH + row_ids % STRETCH
    doc_ends = jnp.cumsum(doc_blocks)
    document = jnp.sum((doc_ends[None, :] <= block_of[:, None]).astype(jnp.int32), axis=1)
    query_all = queries.reshape(TOKENS, KV_HEADS, groups, HEAD_DIM).astype(jnp.float32)
    key_all = keys.reshape(TOKENS, KV_HEADS, HEAD_DIM).astype(jnp.float32)
    value_all = values.reshape(TOKENS, KV_HEADS, HEAD_DIM).astype(jnp.float32)
    grad_all = grad_out.reshape(TOKENS, KV_HEADS, groups, HEAD_DIM).astype(jnp.float32)

    def one_block(totals, block_id):
        key_grad, value_grad = totals
        row_start = (block_id * TOK_DEV).astype(jnp.int32)
        query_rows = lax.dynamic_slice_in_dim(query_all, row_start, TOK_DEV, 0)
        grad_rows = lax.dynamic_slice_in_dim(grad_all, row_start, TOK_DEV, 0)
        pos_rows = lax.dynamic_slice_in_dim(position, row_start, TOK_DEV, 0)
        doc_rows = lax.dynamic_slice_in_dim(document, row_start, TOK_DEV, 0)
        visible = (doc_rows[:, None] == document[None, :]) & (position[None, :] <= pos_rows[:, None])
        scores = jnp.einsum("igqe,jge->gqij", query_rows, key_all) * score_scale
        scores = jnp.where(visible, scores, -jnp.inf)
        row_max = jnp.max(scores, axis=-1)
        log_total = row_max + jnp.log(jnp.sum(jnp.exp(scores - row_max[..., None]), axis=-1))
        probs_full = jnp.exp(scores - log_total[..., None])
        probs_low = lax.optimization_barrier(probs_full.astype(jnp.bfloat16)).astype(jnp.float32)
        output = lax.optimization_barrier(
            jnp.einsum("gqij,jge->igqe", probs_low, value_all).astype(jnp.bfloat16))
        inner_rows = jnp.einsum("igqe,igqe->gqi", grad_rows, output.astype(jnp.float32))
        prob_grad = jnp.einsum("igqe,jge->gqij", grad_rows, value_all)
        score_grad = probs_full * (prob_grad - inner_rows[..., None])
        score_low = lax.optimization_barrier(score_grad.astype(jnp.bfloat16)).astype(jnp.float32)
        query_grad = (score_scale * jnp.einsum("gqij,jge->igqe", score_low, key_all)).astype(jnp.bfloat16)
        key_grad = key_grad + score_scale * jnp.einsum("gqij,igqe->jge", score_low, query_rows)
        value_grad = value_grad + jnp.einsum("gqij,igqe->jge", probs_low, grad_rows)
        return (key_grad, value_grad), (output, query_grad)

    start_totals = (jnp.zeros((TOKENS, KV_HEADS, HEAD_DIM), jnp.float32),
                    jnp.zeros((TOKENS, KV_HEADS, HEAD_DIM), jnp.float32))
    totals, stacked = lax.scan(one_block, start_totals, jnp.arange(N_CTX, dtype=jnp.int32))
    output = stacked[0].reshape(TOKENS, HEADS * HEAD_DIM)
    query_grad = stacked[1].reshape(TOKENS, HEADS * HEAD_DIM)
    key_grad = totals[0].astype(jnp.bfloat16).reshape(TOKENS, KV_HEADS * HEAD_DIM)
    value_grad = totals[1].astype(jnp.bfloat16).reshape(TOKENS, KV_HEADS * HEAD_DIM)
    return (output, query_grad, key_grad, value_grad)
```

```python
import functools

import jax
import jax.numpy as jnp
from jax import lax
from jax.experimental import pallas as pl
from jax.experimental.pallas import tpu as pltpu
from jax.sharding import PartitionSpec as P

HEADS = 32
KV_HEADS = 4
HEAD_DIM = 128
GROUPS = HEADS // KV_HEADS
STRETCH = 64
REACH = 8
WINDOW = (REACH + 1) * STRETCH
ROWS = GROUPS * STRETCH
PAIR = 2 * HEAD_DIM
MESH = pl.DeviceIdType.MESH
SCALE = HEAD_DIM ** (-0.5)
SCALE_LOG2E = SCALE * 1.4426950408889634


def dot_nt(a, b):
    return lax.dot_general(a, b, (((1,), (1,)), ((), ())), preferred_element_type=jnp.float32)


def dot_nn(a, b):
    return lax.dot_general(a, b, (((1,), (0,)), ((), ())), preferred_element_type=jnp.float32)


def when_copy(active, remote, source, target, send_sem, recv_sem, device):
    @pl.when(active & remote)
    def _():
        pltpu.make_async_remote_copy(
            source, target, send_sem, recv_sem, device_id={"ctx": device}, device_id_type=MESH
        ).start()

    @pl.when(active & jnp.logical_not(remote))
    def _():
        pltpu.make_async_copy(source, target, recv_sem).start()


def kernel(
    n, docs_ref, q_ref, k_ref, v_ref, do_ref, o_ref, dq_ref, dk_ref, dv_ref,
    own, win, part, recv, diag, s_ref, dp_ref, p_ref, ds_ref,
    gsend, grecv, rsend, rrecv,
):
    me = lax.axis_index("ctx")
    last = 2 * n - 1

    barrier = pltpu.get_barrier_semaphore()

    @pl.loop(1, n)
    def _(step):
        pl.semaphore_signal(
            barrier, inc=1, device_id={"ctx": lax.rem(me + step, n)}, device_id_type=MESH
        )

    for g in range(KV_HEADS):
        cols = slice(g * HEAD_DIM, (g + 1) * HEAD_DIM)
        for o in range(2):
            rows = slice(o * STRETCH, (o + 1) * STRETCH)
            own[g, o, :, :HEAD_DIM] = k_ref[rows, cols]
            own[g, o, :, HEAD_DIM:] = v_ref[rows, cols]
            win[g, o, REACH * STRETCH :, :HEAD_DIM] = k_ref[rows, cols]
            win[g, o, REACH * STRETCH :, HEAD_DIM:] = v_ref[rows, cols]

    @pl.loop(0, KV_HEADS * REACH)
    def _(turn):
        g, k = turn // REACH, lax.rem(turn, REACH) + 1

        @pl.when(me < k)
        def _():
            row = pl.multiple_of((REACH - k) * STRETCH, STRETCH)
            win[g, 0, pl.ds(row, STRETCH), :] = jnp.zeros((STRETCH, PAIR), jnp.bfloat16)
            recv[g, 1, k - 1] = jnp.zeros((STRETCH, PAIR), jnp.bfloat16)

    pl.semaphore_wait(barrier, n - 1)

    @pl.loop(0, KV_HEADS * REACH)
    def _(turn):
        g, k = turn // REACH, lax.rem(turn, REACH) + 1
        row = pl.multiple_of((REACH - k) * STRETCH, STRETCH)
        low = me + k < n
        reader = jnp.where(low, me + k, last - me - k)
        slot = jnp.where(low, 0, 1)
        when_copy(
            k >= 1, reader != me, own.at[g, 0], win.at[g, slot, pl.ds(row, STRETCH)],
            gsend.at[g, 0, k - 1], grecv.at[g, slot, k - 1], reader,
        )

        @pl.when(me >= k)
        def _():
            pltpu.make_async_remote_copy(
                own.at[g, 1], win.at[g, 1, pl.ds(row, STRETCH)], gsend.at[g, 1, k - 1],
                grecv.at[g, 1, k - 1], device_id={"ctx": me - k}, device_id_type=MESH,
            ).start()

    def doc_start(block):
        end = jnp.int32(0)
        start = jnp.int32(0)
        for d in range(8):
            end = end + docs_ref[d]
            start = jnp.where(end <= block, end, start)
        return start

    col = lax.broadcasted_iota(jnp.int32, (STRETCH, ROWS), 0)
    row_of = lax.rem(lax.broadcasted_iota(jnp.int32, (STRETCH, ROWS), 1), STRETCH)
    later = row_of < col

    def eights(x, op):
        return op(x.reshape(STRETCH // 8, 8, ROWS), axis=0)

    def head_rows(ref, o, g):
        r = pl.multiple_of(o * STRETCH, STRETCH)
        return jnp.concatenate(
            [
                ref[
                    pl.ds(r, STRETCH),
                    pl.ds(pl.multiple_of((g * GROUPS + h) * HEAD_DIM, HEAD_DIM), HEAD_DIM),
                ]
                for h in range(GROUPS)
            ],
            axis=0,
        )

    def put_heads(ref, o, g, value):
        r = pl.multiple_of(o * STRETCH, STRETCH)
        for h in range(GROUPS):
            ref[
                pl.ds(r, STRETCH),
                pl.ds(pl.multiple_of((g * GROUPS + h) * HEAD_DIM, HEAD_DIM), HEAD_DIM),
            ] = value[h * STRETCH : (h + 1) * STRETCH]

    def tile(g, o):
        block = jnp.where(o == 0, me, last - me)
        start = doc_start(block)
        bias = [
            jnp.where(block - (REACH - kb) >= start, jnp.float32(0), jnp.float32(-jnp.inf))
            for kb in range(REACH + 1)
        ]
        q = head_rows(q_ref, o, g)
        do = head_rows(do_ref, o, g)
        keys = win[g, o, :, :HEAD_DIM]
        vals = win[g, o, :, HEAD_DIM:]
        s_ref[...] = dot_nt(keys, q)
        dp_ref[...] = dot_nt(vals, do)
        spans = [slice(kb * STRETCH, (kb + 1) * STRETCH) for kb in range(REACH + 1)]
        on_diag = jnp.where(later, -jnp.inf, s_ref[spans[REACH], :])
        s_ref[spans[REACH], :] = on_diag
        top = eights(on_diag, jnp.max)
        for kb in range(REACH):
            top = jnp.maximum(top, eights(s_ref[spans[kb], :], jnp.max) + bias[kb])
        top = jnp.max(top, axis=0, keepdims=True) * SCALE_LOG2E
        total = jnp.zeros((8, ROWS), jnp.float32)
        inner = jnp.zeros((8, ROWS), jnp.float32)
        for kb in range(REACH + 1):
            e = jnp.exp2(s_ref[spans[kb], :] * SCALE_LOG2E + (bias[kb] - top))
            s_ref[spans[kb], :] = e
            total = total + eights(e, jnp.sum)
            inner = inner + eights(e * dp_ref[spans[kb], :], jnp.sum)
        inverse = 1.0 / jnp.sum(total, axis=0, keepdims=True)
        inner = jnp.sum(inner, axis=0, keepdims=True) * inverse
        for kb in range(REACH + 1):
            p = s_ref[spans[kb], :] * inverse
            p_ref[spans[kb], :] = p.astype(jnp.bfloat16)
            ds_ref[spans[kb], :] = (p * (dp_ref[spans[kb], :] - inner)).astype(jnp.bfloat16)
        put_heads(o_ref, o, g, dot_nn(vals.T, p_ref[...]).astype(jnp.bfloat16).T)
        put_heads(dq_ref, o, g, (SCALE * dot_nn(keys.T, ds_ref[...])).astype(jnp.bfloat16).T)
        dv = dot_nn(p_ref[...], do)
        dk = SCALE * dot_nn(ds_ref[...], q)
        edge = REACH * STRETCH
        part[g, o, :, :HEAD_DIM] = dk[:edge].astype(jnp.bfloat16)
        part[g, o, :, HEAD_DIM:] = dv[:edge].astype(jnp.bfloat16)
        diag[g, o, :, :HEAD_DIM] = dk[edge:]
        diag[g, o, :, HEAD_DIM:] = dv[edge:]

    def gather_wait(g, o, k):
        row = pl.multiple_of((REACH - k) * STRETCH, STRETCH)
        here = pltpu.make_async_copy(
            own.at[g, o], win.at[g, o, pl.ds(row, STRETCH)], grecv.at[g, o, k - 1]
        )

        @pl.when((o == 1) | (me >= k))
        def _():
            here.wait()

    @pl.loop(0, KV_HEADS)
    def _(g):
        @pl.loop(0, 2)
        def _(o):
            @pl.loop(1, REACH + 1)
            def _(k):
                gather_wait(g, o, k)

            tile(g, o)

            @pl.loop(1, REACH + 1)
            def _(k):
                row = pl.multiple_of((REACH - k) * STRETCH, STRETCH)
                high = (o == 1) & (me + k < n)
                home = jnp.where(o == 0, me - k, jnp.where(high, me + k, last - me - k))
                slot = jnp.where(high, 1, 0)
                when_copy(
                    home >= 0, home != me, part.at[g, o, pl.ds(row, STRETCH)],
                    recv.at[g, slot, k - 1], rsend.at[g, o, k - 1], rrecv.at[g, slot, k - 1],
                    home,
                )

    @pl.loop(0, KV_HEADS)
    def _(g):
        cols = pl.ds(pl.multiple_of(g * HEAD_DIM, HEAD_DIM), HEAD_DIM)
        for o in range(2):

            @pl.loop(1, REACH + 1)
            def _(k):
                @pl.when((o == 0) | (me >= k))
                def _():
                    pltpu.make_async_copy(
                        part.at[g, o, pl.ds(0, STRETCH)], recv.at[g, o, k - 1],
                        rrecv.at[g, o, k - 1],
                    ).wait()

            rows = slice(o * STRETCH, (o + 1) * STRETCH)
            acc = diag[g, o]
            for k in range(REACH):
                acc = acc + recv[g, o, k].astype(jnp.float32)
            dk_ref[rows, cols] = acc[:, :HEAD_DIM].astype(jnp.bfloat16)
            dv_ref[rows, cols] = acc[:, HEAD_DIM:].astype(jnp.bfloat16)

    @pl.loop(0, KV_HEADS * REACH)
    def _(turn):
        g, k = turn // REACH, lax.rem(turn, REACH) + 1
        low = me + k < n
        reader = jnp.where(low, me + k, last - me - k)

        @pl.when(reader != me)
        def _():
            pltpu.make_async_copy(own.at[g, 0], own.at[g, 0], gsend.at[g, 0, k - 1]).wait()

        @pl.when(me >= k)
        def _():
            pltpu.make_async_copy(own.at[g, 1], own.at[g, 1], gsend.at[g, 1, k - 1]).wait()
            pltpu.make_async_copy(own.at[g, 0], own.at[g, 0], rsend.at[g, 0, k - 1]).wait()

        @pl.when(last - me - k != me)
        def _():
            pltpu.make_async_copy(own.at[g, 1], own.at[g, 1], rsend.at[g, 1, k - 1]).wait()


def local(queries, keys, values, grad_out, doc_blocks):
    n = lax.axis_size("ctx")
    vmem = pl.BlockSpec(memory_space=pltpu.VMEM)
    bf16, f32 = jnp.bfloat16, jnp.float32
    dma = pltpu.SemaphoreType.DMA((KV_HEADS, 2, REACH))
    return pl.pallas_call(
        functools.partial(kernel, n),
        out_shape=(
            jax.ShapeDtypeStruct(queries.shape, bf16),
            jax.ShapeDtypeStruct(queries.shape, bf16),
            jax.ShapeDtypeStruct(keys.shape, bf16),
            jax.ShapeDtypeStruct(values.shape, bf16),
        ),
        in_specs=[pl.BlockSpec(memory_space=pltpu.SMEM)] + [vmem] * 4,
        out_specs=(vmem,) * 4,
        scratch_shapes=[
            pltpu.VMEM((KV_HEADS, 2, STRETCH, PAIR), bf16),
            pltpu.VMEM((KV_HEADS, 2, WINDOW, PAIR), bf16),
            pltpu.VMEM((KV_HEADS, 2, REACH * STRETCH, PAIR), bf16),
            pltpu.VMEM((KV_HEADS, 2, REACH, STRETCH, PAIR), bf16),
            pltpu.VMEM((KV_HEADS, 2, STRETCH, PAIR), f32),
            pltpu.VMEM((WINDOW, ROWS), f32),
            pltpu.VMEM((WINDOW, ROWS), f32),
            pltpu.VMEM((WINDOW, ROWS), bf16),
            pltpu.VMEM((WINDOW, ROWS), bf16),
            dma, dma, dma, dma,
        ],
        compiler_params=pltpu.CompilerParams(
            collective_id=0, has_side_effects=True, vmem_limit_bytes=48 * 2**20
        ),
    )(doc_blocks, queries, keys, values, grad_out)


def solution(mesh):
    token = P(("dp", "ctx"), None)
    return jax.shard_map(
        local, mesh=mesh, in_specs=(token, token, token, token, P("dp")),
        out_specs=(token,) * 4, check_vma=False,
    )
```

```python
import jax
import jax.numpy as jnp
from jax import lax
from jax.experimental import pallas as pl
from jax.experimental.pallas import tpu as pltpu
from jax.sharding import PartitionSpec as P

HEADS = 32
KV_HEADS = 4
HEAD_DIM = 128
GROUPS = HEADS // KV_HEADS
STRETCH = 64
REACH = 8
WINDOW = (REACH + 1) * STRETCH
ROWS = GROUPS * STRETCH
PAIR = 2 * HEAD_DIM
MESH = pl.DeviceIdType.MESH
SCALE = HEAD_DIM ** (-0.5)
SCALE_LOG2E = SCALE * 1.4426950408889634


def dot_nt(a, b):
    return lax.dot_general(a, b, (((1,), (1,)), ((), ())), preferred_element_type=jnp.float32)


def dot_nn(a, b):
    return lax.dot_general(a, b, (((1,), (0,)), ((), ())), preferred_element_type=jnp.float32)


N, LAST, DEPTH = 16, 31, 3

TREE = (
    (0, 0, 0, 0, 1, 2, 6, 0,),
    (3, 1, 5, 1, 2, 3, 4, 1,),
    (2, 6, 6, 2, 4, 10, 5, 2,),
    (7, 4, 7, 3, 4, 11, 6, 7,),
    (4, 5, 4, 4, 5, 6, 8, 4,),
    (7, 5, 9, 5, 6, 8, 8, 5,),
    (6, 10, 8, 6, 7, 8, 14, 10,),
    (12, 11, 14, 7, 15, 9, 15, 7,),
    (8, 9, 8, 8, 12, 10, 11,),
    (9, 10, 13, 9, 13, 12,),
    (10, 13, 14, 10, 14,),
    (15, 14, 15, 11,),
    (15, 12, 12, 12,),
    (14, 15, 13, 13, 14,),
    (13, 14, 15, 13, 14, 14,),
    (12, 13, 11, 15, 15, 12, 15,),
    (15, 12, 13, 9, 7, 15, 15, 13,),
    (10, 11, 11, 10, 14, 10, 14, 9,),
    (9, 5, 11, 9, 13, 11, 9, 8,),
    (8, 9, 10, 11, 12, 8, 8, 8,),
    (7, 7, 6, 7, 11, 4, 10, 11,),
    (6, 7, 8, 6, 10, 6, 10, 5,),
    (9, 6, 1, 8, 9, 5, 3, 9,),
    (8, 0, 6, 7, 8, 1, 4, 4,),
    (3, 5, 3, 7, 7, 4, 2,),
    (4, 2, 6, 2, 5, 6,),
    (3, 5, 1, 1, 5,),
    (4, 0, 1, 0,),
    (3, 2, 3,),
    (1, 2,),
    (1,),
    (),
)


def holder(block):
    return min(block, LAST - block)


def place(device, block):
    if block in (device, LAST - device):
        return (0, 0) if block == device else (1, 0)
    low = device - block
    return (0, low) if 0 < low <= REACH else (1, LAST - device - block)


class Slot:
    def __init__(self, device, block, level):
        self.o, self.k = place(device, block)
        self.level, self.to, self.source = level, [], None


def build():
    plan = [[] for _ in range(N)]
    count = [0] * N
    for block, parents in enumerate(TREE):
        top = min(block + REACH, LAST)
        readers = sorted({holder(b) for b in range(block + 1, top + 1)} - {holder(block)})
        slots = {holder(block): Slot(holder(block), block, 0)}
        left = dict(zip(readers, parents, strict=True))
        while left:
            for device, source in sorted(left.items()):
                if source in slots and device not in slots and slots[source].level < DEPTH:
                    slots[device] = Slot(device, block, slots[source].level + 1)
                    slots[device].source = (source, count[source])
                    slots[source].to.append((device, count[source], slots[device]))
                    count[source] += 1
                    del left[device]
        for device, slot in slots.items():
            plan[device].append(slot)
    return plan, max(count)


PLAN, HOPS = build()
NEAR = [
    sorted(
        {hop[0] for slot in slots for hop in slot.to}
        | {slot.source[0] for slot in slots if slot.source}
    )
    for slots in PLAN
]


def each_device(me, emit):
    for device in range(N):

        @pl.when(me == device)
        def _():
            emit(device)


def span(k):
    return slice((REACH - k) * STRETCH, (REACH - k + 1) * STRETCH)


def kernel(
    docs_hbm, q_hbm, k_hbm, v_hbm, do_hbm, o_hbm, dq_hbm, dk_hbm, dv_hbm,
    docs, q_buf, k_buf, v_buf, do_buf, o_buf, dq_buf, dk_buf, dv_buf, win, part, diag, coming,
    s_ref, dp_ref, p_ref, ds_ref, fetch, store, keep, gsend, grecv, rsend, rrecv,
):
    me = lax.axis_index("ctx")
    last = LAST

    fetches = [
        pltpu.make_async_copy(a, b, fetch.at[i])
        for i, (a, b) in enumerate(
            [(k_hbm, k_buf), (v_hbm, v_buf), (docs_hbm, docs), (q_hbm, q_buf), (do_hbm, do_buf)]
        )
    ]
    for copy in fetches:
        copy.start()

    barrier = pltpu.get_barrier_semaphore()

    def greet(device):
        for near in NEAR[device]:
            pl.semaphore_signal(barrier, inc=1, device_id={"ctx": near}, device_id_type=MESH)

    each_device(me, greet)
    fetches[0].wait()
    fetches[1].wait()
    for g in range(KV_HEADS):
        cols = slice(g * HEAD_DIM, (g + 1) * HEAD_DIM)
        for o in range(2):
            rows = slice(o * STRETCH, (o + 1) * STRETCH)
            win[g, o, span(0), :HEAD_DIM] = k_buf[rows, cols]
            win[g, o, span(0), HEAD_DIM:] = v_buf[rows, cols]

    @pl.loop(0, KV_HEADS)
    def _(g):
        for k in range(1, REACH + 1):

            @pl.when(me < k)
            def _():
                win[g, 0, span(k), :] = jnp.zeros((STRETCH, PAIR), jnp.bfloat16)

    each_device(me, lambda device: pl.semaphore_wait(barrier, len(NEAR[device])))

    def arrived(g, slot):
        here = win.at[g, slot.o, span(slot.k)]
        pltpu.make_async_copy(here, here, grecv.at[g, slot.o, slot.k - 1]).wait()

    def spread(level, g):
        def emit(device):
            for slot in PLAN[device]:
                if slot.level != level or not slot.to:
                    continue
                if slot.k:
                    arrived(g, slot)
                for there, e, other in slot.to:
                    pltpu.make_async_remote_copy(
                        win.at[g, slot.o, span(slot.k)], win.at[g, other.o, span(other.k)],
                        gsend.at[g, e], grecv.at[g, other.o, other.k - 1],
                        device_id={"ctx": there}, device_id_type=MESH,
                    ).start()

        each_device(me, emit)

    def twins(device):
        base = last - 2 * device
        return [(k, k + base) for k in range(REACH + 1) if k <= device and k + base <= REACH]

    def complete(g):
        def emit(device):
            for slot in PLAN[device]:
                if slot.k and not slot.to:
                    arrived(g, slot)
            for low, high in twins(device):
                win[g, 1, span(high), :] = win[g, 0, span(low), :]

        each_device(me, emit)

    def doc_start(block):
        end = jnp.int32(0)
        start = jnp.int32(0)
        for d in range(8):
            end = end + docs[d]
            start = jnp.where(end <= block, end, start)
        return start

    col = lax.broadcasted_iota(jnp.int32, (STRETCH, ROWS), 0)
    row_of = lax.rem(lax.broadcasted_iota(jnp.int32, (STRETCH, ROWS), 1), STRETCH)
    later = row_of < col

    def eights(x, op):
        return op(x.reshape(STRETCH // 8, 8, ROWS), axis=0)

    def head_rows(ref, o, g):
        r = pl.multiple_of(o * STRETCH, STRETCH)
        return jnp.concatenate(
            [
                ref[
                    pl.ds(r, STRETCH),
                    pl.ds(pl.multiple_of((g * GROUPS + h) * HEAD_DIM, HEAD_DIM), HEAD_DIM),
                ]
                for h in range(GROUPS)
            ],
            axis=0,
        )

    def put_heads(ref, o, g, value):
        r = pl.multiple_of(o * STRETCH, STRETCH)
        for h in range(GROUPS):
            ref[
                pl.ds(r, STRETCH),
                pl.ds(pl.multiple_of((g * GROUPS + h) * HEAD_DIM, HEAD_DIM), HEAD_DIM),
            ] = value[h * STRETCH : (h + 1) * STRETCH]

    def stores(g, o):
        rows = pl.ds(pl.multiple_of(o * STRETCH, STRETCH), STRETCH)
        width = GROUPS * HEAD_DIM
        cols = pl.ds(pl.multiple_of(g * width, width), width)
        return [
            pltpu.make_async_copy(a.at[rows, cols], b.at[rows, cols], store.at[i, g, o])
            for i, (a, b) in enumerate([(o_buf, o_hbm), (dq_buf, dq_hbm)])
        ]

    def keeps(g):
        cols = pl.ds(pl.multiple_of(g * HEAD_DIM, HEAD_DIM), HEAD_DIM)
        return [
            pltpu.make_async_copy(a.at[:, cols], b.at[:, cols], keep.at[i, g])
            for i, (a, b) in enumerate([(dk_buf, dk_hbm), (dv_buf, dv_hbm)])
        ]

    def tile(g, o):
        block = jnp.where(o == 0, me, last - me)
        start = doc_start(block)
        bias = [
            jnp.where(block - (REACH - kb) >= start, jnp.float32(0), jnp.float32(-jnp.inf))
            for kb in range(REACH + 1)
        ]
        q = head_rows(q_buf, o, g)
        do = head_rows(do_buf, o, g)
        keys = win[g, o, :, :HEAD_DIM]
        vals = win[g, o, :, HEAD_DIM:]
        s_ref[...] = dot_nt(keys, q)
        dp_ref[...] = dot_nt(vals, do)
        spans = [slice(kb * STRETCH, (kb + 1) * STRETCH) for kb in range(REACH + 1)]
        on_diag = jnp.where(later, -jnp.inf, s_ref[spans[REACH], :])
        s_ref[spans[REACH], :] = on_diag
        top = eights(on_diag, jnp.max)
        for kb in range(REACH):
            top = jnp.maximum(top, eights(s_ref[spans[kb], :], jnp.max) + bias[kb])
        top = jnp.max(top, axis=0, keepdims=True) * SCALE_LOG2E
        total = jnp.zeros((8, ROWS), jnp.float32)
        inner = jnp.zeros((8, ROWS), jnp.float32)
        for kb in range(REACH + 1):
            e = jnp.exp2(s_ref[spans[kb], :] * SCALE_LOG2E + (bias[kb] - top))
            s_ref[spans[kb], :] = e
            total = total + eights(e, jnp.sum)
            inner = inner + eights(e * dp_ref[spans[kb], :], jnp.sum)
        inverse = 1.0 / jnp.sum(total, axis=0, keepdims=True)
        inner = jnp.sum(inner, axis=0, keepdims=True) * inverse
        for kb in range(REACH + 1):
            p = s_ref[spans[kb], :] * inverse
            p_ref[spans[kb], :] = p.astype(jnp.bfloat16)
            ds_ref[spans[kb], :] = (p * (dp_ref[spans[kb], :] - inner)).astype(jnp.bfloat16)
        put_heads(o_buf, o, g, dot_nn(vals.T, p_ref[...]).astype(jnp.bfloat16).T)
        put_heads(dq_buf, o, g, (SCALE * dot_nn(keys.T, ds_ref[...])).astype(jnp.bfloat16).T)
        dv = dot_nn(p_ref[...], do)
        dk = SCALE * dot_nn(ds_ref[...], q)
        edge = REACH * STRETCH
        part[g, o, :edge, :HEAD_DIM] = dk[:edge].astype(jnp.bfloat16)
        part[g, o, :edge, HEAD_DIM:] = dv[:edge].astype(jnp.bfloat16)
        diag[g, o, :, :HEAD_DIM] = dk[edge:]
        diag[g, o, :, HEAD_DIM:] = dv[edge:]
        for copy in stores(g, o):
            copy.start()

    def send_home(g, device, slot):
        there, e = slot.source
        pltpu.make_async_remote_copy(
            part.at[g, slot.o, span(slot.k)], coming.at[g, e],
            rsend.at[g, slot.o, slot.k - 1], rrecv.at[g, e],
            device_id={"ctx": there}, device_id_type=MESH,
        ).start()

    def leaves(g, o):
        def emit(device):
            if o == 0:
                for low, high in twins(device):
                    twin = part[g, 1, span(high), :].astype(jnp.float32)
                    if low:
                        total = part[g, 0, span(low), :].astype(jnp.float32) + twin
                        part[g, 0, span(low), :] = total.astype(jnp.bfloat16)
                    else:
                        diag[g, 0] = diag[g, 0] + twin
            for slot in sorted(PLAN[device], key=lambda slot: -slot.level):
                if slot.k and slot.o == o and not slot.to:
                    send_home(g, device, slot)

        each_device(me, emit)

    def collect(level, g):
        def emit(device):
            for slot in PLAN[device]:
                if slot.level != level or not slot.to:
                    continue
                for _, e, _ in slot.to:
                    there = coming.at[g, e]
                    pltpu.make_async_copy(there, there, rrecv.at[g, e]).wait()
                if slot.k:
                    total = part[g, slot.o, span(slot.k), :].astype(jnp.float32)
                else:
                    total = diag[g, slot.o]
                for _, e, _ in slot.to:
                    total = total + coming[g, e].astype(jnp.float32)
                if slot.k:
                    part[g, slot.o, span(slot.k), :] = total.astype(jnp.bfloat16)
                    send_home(g, device, slot)
                else:
                    diag[g, slot.o] = total

        each_device(me, emit)
        if level == 0:
            cols = pl.ds(pl.multiple_of(g * HEAD_DIM, HEAD_DIM), HEAD_DIM)
            for o in range(2):
                rows = slice(o * STRETCH, (o + 1) * STRETCH)
                dk_buf[rows, cols] = diag[g, o, :, :HEAD_DIM].astype(jnp.bfloat16)
                dv_buf[rows, cols] = diag[g, o, :, HEAD_DIM:].astype(jnp.bfloat16)
            for copy in keeps(g):
                copy.start()

    tiles = 2 * KV_HEADS

    @pl.loop(-KV_HEADS, tiles + 2 * DEPTH)
    def _(turn):
        for level in range(DEPTH):
            g = turn + (KV_HEADS if level == 0 else DEPTH - level)

            @pl.when((g >= 0) & (g < KV_HEADS))
            def _():
                spread(level, g)

        @pl.when(turn == 0)
        def _():
            for copy in fetches[2:]:
                copy.wait()

        @pl.when((turn >= 0) & (turn < tiles))
        def _():
            g, second = turn // 2, lax.rem(turn, 2) == 0

            @pl.when(second)
            def _():
                complete(g)

            tile(g, jnp.where(second, 1, 0))

            @pl.when(second)
            def _():
                leaves(g, 1)

            @pl.when(jnp.logical_not(second))
            def _():
                leaves(g, 0)

        for level in range(DEPTH):
            since = turn - 1 - 2 * (DEPTH - level)

            @pl.when((since >= 0) & (lax.rem(since, 2) == 0) & (since < tiles))
            def _():
                collect(level, since // 2)

    @pl.loop(0, KV_HEADS)
    def _(g):
        def emit(device):
            for slot in PLAN[device]:
                for _, e, _ in slot.to:
                    here = win.at[g, 0, span(0)]
                    pltpu.make_async_copy(here, here, gsend.at[g, e]).wait()
                if slot.k:
                    here = part.at[g, slot.o, span(slot.k)]
                    pltpu.make_async_copy(here, here, rsend.at[g, slot.o, slot.k - 1]).wait()

        each_device(me, emit)
        for copy in stores(g, 0) + stores(g, 1) + keeps(g):
            copy.wait()


PIECES = 4


def hand_over(*refs):
    arrays, results, bufs, (arrive, leave) = refs[:4], refs[4:8], refs[8:12], refs[12:]
    inward, outward = [], []
    for i, (a, b, buf) in enumerate(zip(arrays, results, bufs, strict=True)):
        rows = a.shape[0] // PIECES
        for j in range(PIECES):
            piece = slice(j * rows, (j + 1) * rows)
            inward.append(pltpu.make_async_copy(a.at[piece], buf.at[piece], arrive.at[i, j]))
            outward.append(pltpu.make_async_copy(buf.at[piece], b.at[piece], leave.at[i, j]))
    for copy in inward:
        copy.start()
    for copy, after in zip(inward, outward, strict=True):
        copy.wait()
        after.start()
    for copy in outward:
        copy.wait()


def local(queries, keys, values, grad_out, doc_blocks):
    hbm = pl.BlockSpec(memory_space=pltpu.HBM)
    bf16, f32 = jnp.bfloat16, jnp.float32
    edge = pltpu.SemaphoreType.DMA((KV_HEADS, HOPS))
    slot = pltpu.SemaphoreType.DMA((KV_HEADS, 2, REACH))
    shapes = (
        jax.ShapeDtypeStruct(queries.shape, bf16),
        jax.ShapeDtypeStruct(queries.shape, bf16),
        jax.ShapeDtypeStruct(keys.shape, bf16),
        jax.ShapeDtypeStruct(values.shape, bf16),
    )
    results = pl.pallas_call(
        kernel,
        out_shape=shapes,
        in_specs=[hbm] * 5,
        out_specs=(hbm,) * 4,
        scratch_shapes=[
            pltpu.SMEM(doc_blocks.shape, jnp.int32),
            pltpu.VMEM(queries.shape, bf16),
            pltpu.VMEM(keys.shape, bf16),
            pltpu.VMEM(values.shape, bf16),
            pltpu.VMEM(queries.shape, bf16),
            pltpu.VMEM(queries.shape, bf16),
            pltpu.VMEM(queries.shape, bf16),
            pltpu.VMEM(keys.shape, bf16),
            pltpu.VMEM(values.shape, bf16),
            pltpu.VMEM((KV_HEADS, 2, WINDOW, PAIR), bf16),
            pltpu.VMEM((KV_HEADS, 2, REACH * STRETCH, PAIR), bf16),
            pltpu.VMEM((KV_HEADS, 2, STRETCH, PAIR), f32),
            pltpu.VMEM((KV_HEADS, HOPS, STRETCH, PAIR), bf16),
            pltpu.VMEM((WINDOW, ROWS), f32),
            pltpu.VMEM((WINDOW, ROWS), f32),
            pltpu.VMEM((WINDOW, ROWS), bf16),
            pltpu.VMEM((WINDOW, ROWS), bf16),
            pltpu.SemaphoreType.DMA((5,)),
            pltpu.SemaphoreType.DMA((2, KV_HEADS, 2)),
            pltpu.SemaphoreType.DMA((2, KV_HEADS)),
            edge, slot, slot, edge,
        ],
        compiler_params=pltpu.CompilerParams(
            collective_id=0, has_side_effects=True, vmem_limit_bytes=60 * 2**20
        ),
    )(doc_blocks, queries, keys, values, grad_out)
    return pl.pallas_call(
        hand_over,
        out_shape=shapes,
        in_specs=[hbm] * 4,
        out_specs=(hbm,) * 4,
        scratch_shapes=[pltpu.VMEM(a.shape, bf16) for a in shapes]
        + [pltpu.SemaphoreType.DMA((4, PIECES))] * 2,
        compiler_params=pltpu.CompilerParams(vmem_limit_bytes=60 * 2**20),
    )(*results)


def solution(mesh):
    token = P(("dp", "ctx"), None)
    return jax.shard_map(
        local, mesh=mesh, in_specs=(token, token, token, token, P("dp")),
        out_specs=(token,) * 4, check_vma=False,
    )
```

```python
import jax
import jax.numpy as jnp
from jax import lax
from jax.experimental import pallas as pl
from jax.experimental.pallas import tpu as pltpu
from jax.sharding import PartitionSpec as P

HEADS = 32
KV_HEADS = 4
HEAD_DIM = 128
GROUPS = HEADS // KV_HEADS
STRETCH = 64
REACH = 8
WINDOW = (REACH + 1) * STRETCH
ROWS = GROUPS * STRETCH
PAIR = 2 * HEAD_DIM
MESH = pl.DeviceIdType.MESH
SCALE = HEAD_DIM ** (-0.5)
SCALE_LOG2E = SCALE * 1.4426950408889634


def dot_nt(a, b):
    return lax.dot_general(a, b, (((1,), (1,)), ((), ())), preferred_element_type=jnp.float32)


def dot_nn(a, b):
    return lax.dot_general(a, b, (((1,), (0,)), ((), ())), preferred_element_type=jnp.float32)


N, LAST = 16, 31

DOWN = (
    (0, 1, 7, 0, 1, 2, 4, 4,),
    (1, 2, 5, 1, 5, 3, 9, 5,),
    (2, 7, 6, 2, 3, 4, 5, 9,),
    (5, 6, 7, 3, 11, 5, 6, 7,),
    (4, 10, 4, 4, 8, 9, 8, 8,),
    (10, 11, 9, 5, 9, 10, 8, 9,),
    (6, 9, 10, 6, 7, 13, 9, 10,),
    (11, 8, 11, 7, 8, 14, 10, 12,),
    (8, 14, 8, 8, 12, 13, 14,),
    (9, 10, 13, 9, 13, 12,),
    (10, 15, 12, 10, 11,),
    (15, 12, 15, 11,),
    (15, 12, 15, 12,),
    (14, 15, 13, 13, 12,),
    (10, 14, 15, 15, 9, 14,),
    (11, 8, 14, 15, 13, 14, 15,),
    (11, 12, 8, 11, 15, 15, 12, 10,),
    (10, 11, 12, 13, 14, 10, 13, 14,),
    (9, 5, 6, 9, 13, 9, 8, 8,),
    (8, 4, 5, 4, 12, 5, 11, 8,),
    (7, 8, 6, 7, 11, 11, 8, 6,),
    (6, 7, 7, 9, 10, 6, 4, 10,),
    (5, 6, 2, 5, 9, 5, 6, 9,),
    (1, 5, 1, 7, 8, 4, 7, 4,),
    (4, 0, 3, 7, 7, 1, 2,),
    (3, 2, 6, 2, 0, 6,),
    (1, 5, 3, 0, 5,),
    (4, 0, 3, 0,),
    (3, 2, 3,),
    (1, 2,),
    (1,),
    (),
)
UP = (
    (2, 3, 0, 0, 4, 2, 3, 4,),
    (1, 2, 5, 1, 5, 4, 9, 5,),
    (2, 7, 6, 2, 3, 4, 10, 6,),
    (7, 6, 7, 3, 4, 5, 11, 7,),
    (4, 5, 6, 4, 5, 11, 8, 8,),
    (5, 6, 9, 5, 6, 8, 13, 9,),
    (11, 9, 10, 6, 10, 13, 14, 10,),
    (11, 8, 11, 7, 8, 12, 10, 11,),
    (8, 9, 10, 8, 12, 13, 14,),
    (9, 15, 13, 9, 15, 12,),
    (10, 15, 14, 10, 11,),
    (15, 12, 15, 11,),
    (15, 14, 15, 12,),
    (14, 15, 13, 13, 14,),
    (13, 9, 15, 13, 14, 14,),
    (12, 13, 14, 8, 15, 14, 15,),
    (11, 11, 8, 11, 15, 15, 12, 13,),
    (10, 6, 12, 8, 14, 10, 13, 14,),
    (6, 10, 6, 12, 13, 9, 10, 13,),
    (7, 9, 7, 11, 12, 8, 9, 8,),
    (7, 7, 4, 7, 11, 9, 10, 11,),
    (6, 7, 8, 4, 10, 6, 9, 10,),
    (5, 1, 7, 8, 9, 7, 4, 9,),
    (4, 5, 1, 0, 8, 4, 7, 4,),
    (3, 2, 6, 2, 5, 6, 7,),
    (3, 0, 6, 2, 0, 6,),
    (1, 5, 1, 2, 5,),
    (4, 2, 3, 0,),
    (3, 0, 3,),
    (1, 2,),
    (1,),
    (),
)
DOWN_TURNS = (8, 5, 3, 1)
UP_TURNS = (17, 12, 6, 2)


def holder(block):
    return min(block, LAST - block)


def place(device, block):
    if block in (device, LAST - device):
        return (0, 0) if block == device else (1, 0)
    low = device - block
    return (0, low) if 0 < low <= REACH else (1, LAST - device - block)


class Slot:
    def __init__(self, device, block, level):
        self.o, self.k = place(device, block)
        self.level, self.to, self.source = level, [], None


def build(tree):
    plan = [[] for _ in range(N)]
    count = [0] * N
    for block, parents in enumerate(tree):
        top = min(block + REACH, LAST)
        readers = sorted({holder(b) for b in range(block + 1, top + 1)} - {holder(block)})
        source = dict(zip(readers, parents, strict=True))
        level = {holder(block): 0}
        while len(level) <= len(readers):
            for device in readers:
                if device not in level and source[device] in level:
                    level[device] = level[source[device]] + 1
        slots = {}
        for device in sorted(level, key=lambda device: (level[device], device)):
            slots[device] = slot = Slot(device, block, level[device])
            plan[device].append(slot)
            if slot.level:
                near = source[device]
                slot.source = (near, count[near])
                slots[near].to.append((device, count[near], slot))
                count[near] += 1
    return plan, max(count)


(DOWN_PLAN, DOWN_HOPS), (UP_PLAN, UP_HOPS) = build(DOWN), build(UP)
NEAR = [
    sorted(
        {hop[0] for slot in down + up for hop in slot.to}
        | {slot.source[0] for slot in down + up if slot.source}
    )
    for down, up in zip(DOWN_PLAN, UP_PLAN, strict=True)
]


def each_device(me, emit):
    for device in range(N):

        @pl.when(me == device)
        def _():
            emit(device)


def span(k):
    return slice((REACH - k) * STRETCH, (REACH - k + 1) * STRETCH)


def kernel(
    docs_hbm, q_hbm, k_hbm, v_hbm, do_hbm, o_hbm, dq_hbm, dk_hbm, dv_hbm,
    docs, q_buf, k_buf, v_buf, do_buf, o_buf, dq_buf, dk_buf, dv_buf, win, part, diag, coming,
    s_ref, dp_ref, p_ref, ds_ref, fetch, store, keep, gsend, grecv, rsend, rrecv,
):
    me = lax.axis_index("ctx")
    last = LAST

    fetches = [
        pltpu.make_async_copy(a, b, fetch.at[i])
        for i, (a, b) in enumerate(
            [(k_hbm, k_buf), (v_hbm, v_buf), (docs_hbm, docs), (q_hbm, q_buf), (do_hbm, do_buf)]
        )
    ]
    for copy in fetches:
        copy.start()

    barrier = pltpu.get_barrier_semaphore()

    def greet(device):
        for near in NEAR[device]:
            pl.semaphore_signal(barrier, inc=1, device_id={"ctx": near}, device_id_type=MESH)

    each_device(me, greet)
    fetches[0].wait()
    fetches[1].wait()
    for g in range(KV_HEADS):
        cols = slice(g * HEAD_DIM, (g + 1) * HEAD_DIM)
        for o in range(2):
            rows = slice(o * STRETCH, (o + 1) * STRETCH)
            win[g, o, span(0), :HEAD_DIM] = k_buf[rows, cols]
            win[g, o, span(0), HEAD_DIM:] = v_buf[rows, cols]

    @pl.loop(0, KV_HEADS)
    def _(g):
        for k in range(1, REACH + 1):

            @pl.when(me < k)
            def _():
                win[g, 0, span(k), :] = jnp.zeros((STRETCH, PAIR), jnp.bfloat16)

    each_device(me, lambda device: pl.semaphore_wait(barrier, len(NEAR[device])))

    def arrived(g, slot):
        here = win.at[g, slot.o, span(slot.k)]
        pltpu.make_async_copy(here, here, grecv.at[g, slot.o, slot.k - 1]).wait()

    def spread(level, g):
        def emit(device):
            for slot in DOWN_PLAN[device]:
                if slot.level != level or not slot.to:
                    continue
                if slot.k:
                    arrived(g, slot)
                for there, e, other in slot.to:
                    pltpu.make_async_remote_copy(
                        win.at[g, slot.o, span(slot.k)], win.at[g, other.o, span(other.k)],
                        gsend.at[g, e], grecv.at[g, other.o, other.k - 1],
                        device_id={"ctx": there}, device_id_type=MESH,
                    ).start()

        each_device(me, emit)

    def twins(device):
        base = last - 2 * device
        return [(k, k + base) for k in range(REACH + 1) if k <= device and k + base <= REACH]

    def complete(g):
        def emit(device):
            for slot in DOWN_PLAN[device]:
                if slot.k and not slot.to:
                    arrived(g, slot)
            for low, high in twins(device):
                win[g, 1, span(high), :] = win[g, 0, span(low), :]

        each_device(me, emit)

    def doc_start(block):
        end = jnp.int32(0)
        start = jnp.int32(0)
        for d in range(8):
            end = end + docs[d]
            start = jnp.where(end <= block, end, start)
        return start

    col = lax.broadcasted_iota(jnp.int32, (STRETCH, ROWS), 0)
    row_of = lax.rem(lax.broadcasted_iota(jnp.int32, (STRETCH, ROWS), 1), STRETCH)
    later = row_of < col

    def eights(x, op):
        return op(x.reshape(STRETCH // 8, 8, ROWS), axis=0)

    def head_rows(ref, o, g):
        r = pl.multiple_of(o * STRETCH, STRETCH)
        return jnp.concatenate(
            [
                ref[
                    pl.ds(r, STRETCH),
                    pl.ds(pl.multiple_of((g * GROUPS + h) * HEAD_DIM, HEAD_DIM), HEAD_DIM),
                ]
                for h in range(GROUPS)
            ],
            axis=0,
        )

    def put_heads(ref, o, g, value):
        r = pl.multiple_of(o * STRETCH, STRETCH)
        for h in range(GROUPS):
            ref[
                pl.ds(r, STRETCH),
                pl.ds(pl.multiple_of((g * GROUPS + h) * HEAD_DIM, HEAD_DIM), HEAD_DIM),
            ] = value[h * STRETCH : (h + 1) * STRETCH]

    def stores(g, o):
        rows = pl.ds(pl.multiple_of(o * STRETCH, STRETCH), STRETCH)
        width = GROUPS * HEAD_DIM
        cols = pl.ds(pl.multiple_of(g * width, width), width)
        return [
            pltpu.make_async_copy(a.at[rows, cols], b.at[rows, cols], store.at[i, g, o])
            for i, (a, b) in enumerate([(o_buf, o_hbm), (dq_buf, dq_hbm)])
        ]

    def keeps(g):
        cols = pl.ds(pl.multiple_of(g * HEAD_DIM, HEAD_DIM), HEAD_DIM)
        return [
            pltpu.make_async_copy(a.at[:, cols], b.at[:, cols], keep.at[i, g])
            for i, (a, b) in enumerate([(dk_buf, dk_hbm), (dv_buf, dv_hbm)])
        ]

    def tile(g, o):
        block = jnp.where(o == 0, me, last - me)
        start = doc_start(block)
        bias = [
            jnp.where(block - (REACH - kb) >= start, jnp.float32(0), jnp.float32(-jnp.inf))
            for kb in range(REACH + 1)
        ]
        q = head_rows(q_buf, o, g)
        do = head_rows(do_buf, o, g)
        keys = win[g, o, :, :HEAD_DIM]
        vals = win[g, o, :, HEAD_DIM:]
        s_ref[...] = dot_nt(keys, q)
        dp_ref[...] = dot_nt(vals, do)
        spans = [slice(kb * STRETCH, (kb + 1) * STRETCH) for kb in range(REACH + 1)]
        on_diag = jnp.where(later, -jnp.inf, s_ref[spans[REACH], :])
        s_ref[spans[REACH], :] = on_diag
        top = eights(on_diag, jnp.max)
        for kb in range(REACH):
            top = jnp.maximum(top, eights(s_ref[spans[kb], :], jnp.max) + bias[kb])
        top = jnp.max(top, axis=0, keepdims=True) * SCALE_LOG2E
        total = jnp.zeros((8, ROWS), jnp.float32)
        inner = jnp.zeros((8, ROWS), jnp.float32)
        for kb in range(REACH + 1):
            e = jnp.exp2(s_ref[spans[kb], :] * SCALE_LOG2E + (bias[kb] - top))
            s_ref[spans[kb], :] = e
            total = total + eights(e, jnp.sum)
            inner = inner + eights(e * dp_ref[spans[kb], :], jnp.sum)
        inverse = 1.0 / jnp.sum(total, axis=0, keepdims=True)
        inner = jnp.sum(inner, axis=0, keepdims=True) * inverse
        for kb in range(REACH + 1):
            p = s_ref[spans[kb], :] * inverse
            p_ref[spans[kb], :] = p.astype(jnp.bfloat16)
            ds_ref[spans[kb], :] = (p * (dp_ref[spans[kb], :] - inner)).astype(jnp.bfloat16)
        put_heads(o_buf, o, g, dot_nn(vals.T, p_ref[...]).astype(jnp.bfloat16).T)
        put_heads(dq_buf, o, g, (SCALE * dot_nn(keys.T, ds_ref[...])).astype(jnp.bfloat16).T)
        dv = dot_nn(p_ref[...], do)
        dk = SCALE * dot_nn(ds_ref[...], q)
        edge = REACH * STRETCH
        part[g, o, :edge, :HEAD_DIM] = dk[:edge].astype(jnp.bfloat16)
        part[g, o, :edge, HEAD_DIM:] = dv[:edge].astype(jnp.bfloat16)
        diag[g, o, :, :HEAD_DIM] = dk[edge:]
        diag[g, o, :, HEAD_DIM:] = dv[edge:]
        for copy in stores(g, o):
            copy.start()

    def send_home(g, device, slot):
        there, e = slot.source
        pltpu.make_async_remote_copy(
            part.at[g, slot.o, span(slot.k)], coming.at[g, e],
            rsend.at[g, slot.o, slot.k - 1], rrecv.at[g, e],
            device_id={"ctx": there}, device_id_type=MESH,
        ).start()

    def leaves(g, o):
        def emit(device):
            if o == 0:
                for low, high in twins(device):
                    twin = part[g, 1, span(high), :].astype(jnp.float32)
                    if low:
                        total = part[g, 0, span(low), :].astype(jnp.float32) + twin
                        part[g, 0, span(low), :] = total.astype(jnp.bfloat16)
                    else:
                        diag[g, 0] = diag[g, 0] + twin
            for slot in sorted(UP_PLAN[device], key=lambda slot: -slot.level):
                if slot.k and slot.o == o and not slot.to:
                    send_home(g, device, slot)

        each_device(me, emit)

    def collect(level, g):
        def emit(device):
            for slot in UP_PLAN[device]:
                if slot.level != level or not slot.to:
                    continue
                for _, e, _ in slot.to:
                    there = coming.at[g, e]
                    pltpu.make_async_copy(there, there, rrecv.at[g, e]).wait()
                if slot.k:
                    total = part[g, slot.o, span(slot.k), :].astype(jnp.float32)
                else:
                    total = diag[g, slot.o]
                for _, e, _ in slot.to:
                    total = total + coming[g, e].astype(jnp.float32)
                if slot.k:
                    part[g, slot.o, span(slot.k), :] = total.astype(jnp.bfloat16)
                    send_home(g, device, slot)
                else:
                    diag[g, slot.o] = total

        each_device(me, emit)
        if level == 0:
            cols = pl.ds(pl.multiple_of(g * HEAD_DIM, HEAD_DIM), HEAD_DIM)
            for o in range(2):
                rows = slice(o * STRETCH, (o + 1) * STRETCH)
                dk_buf[rows, cols] = diag[g, o, :, :HEAD_DIM].astype(jnp.bfloat16)
                dv_buf[rows, cols] = diag[g, o, :, HEAD_DIM:].astype(jnp.bfloat16)
            for copy in keeps(g):
                copy.start()

    tiles = 2 * KV_HEADS

    @pl.loop(-max(DOWN_TURNS), tiles + max(UP_TURNS))
    def _(turn):
        for level, ahead in enumerate(DOWN_TURNS):
            g = turn + ahead

            @pl.when((g >= 0) & (g < KV_HEADS))
            def _():
                spread(level, g)

        @pl.when(turn == 0)
        def _():
            for copy in fetches[2:]:
                copy.wait()

        @pl.when((turn >= 0) & (turn < tiles))
        def _():
            g, second = turn // 2, lax.rem(turn, 2) == 0

            @pl.when(second)
            def _():
                complete(g)

            tile(g, jnp.where(second, 1, 0))

            @pl.when(second)
            def _():
                leaves(g, 1)

            @pl.when(jnp.logical_not(second))
            def _():
                leaves(g, 0)

        for level, behind in enumerate(UP_TURNS):
            since = turn - 1 - behind

            @pl.when((since >= 0) & (lax.rem(since, 2) == 0) & (since < tiles))
            def _():
                collect(level, since // 2)

    @pl.loop(0, KV_HEADS)
    def _(g):
        def emit(device):
            for slot in DOWN_PLAN[device]:
                for _, e, _ in slot.to:
                    here = win.at[g, 0, span(0)]
                    pltpu.make_async_copy(here, here, gsend.at[g, e]).wait()
            for slot in UP_PLAN[device]:
                if slot.k:
                    here = part.at[g, slot.o, span(slot.k)]
                    pltpu.make_async_copy(here, here, rsend.at[g, slot.o, slot.k - 1]).wait()

        each_device(me, emit)
        for copy in stores(g, 0) + stores(g, 1) + keeps(g):
            copy.wait()


PIECES = 4


def hand_over(*refs):
    arrays, results, bufs, (arrive, leave) = refs[:4], refs[4:8], refs[8:12], refs[12:]
    inward, outward = [], []
    for i, (a, b, buf) in enumerate(zip(arrays, results, bufs, strict=True)):
        rows = a.shape[0] // PIECES
        for j in range(PIECES):
            piece = slice(j * rows, (j + 1) * rows)
            inward.append(pltpu.make_async_copy(a.at[piece], buf.at[piece], arrive.at[i, j]))
            outward.append(pltpu.make_async_copy(buf.at[piece], b.at[piece], leave.at[i, j]))
    for copy in inward:
        copy.start()
    for copy, after in zip(inward, outward, strict=True):
        copy.wait()
        after.start()
    for copy in outward:
        copy.wait()


def local(queries, keys, values, grad_out, doc_blocks):
    hbm = pl.BlockSpec(memory_space=pltpu.HBM)
    bf16, f32 = jnp.bfloat16, jnp.float32
    down = pltpu.SemaphoreType.DMA((KV_HEADS, DOWN_HOPS))
    up = pltpu.SemaphoreType.DMA((KV_HEADS, UP_HOPS))
    slot = pltpu.SemaphoreType.DMA((KV_HEADS, 2, REACH))
    shapes = (
        jax.ShapeDtypeStruct(queries.shape, bf16),
        jax.ShapeDtypeStruct(queries.shape, bf16),
        jax.ShapeDtypeStruct(keys.shape, bf16),
        jax.ShapeDtypeStruct(values.shape, bf16),
    )
    results = pl.pallas_call(
        kernel,
        out_shape=shapes,
        in_specs=[hbm] * 5,
        out_specs=(hbm,) * 4,
        scratch_shapes=[
            pltpu.SMEM(doc_blocks.shape, jnp.int32),
            pltpu.VMEM(queries.shape, bf16),
            pltpu.VMEM(keys.shape, bf16),
            pltpu.VMEM(values.shape, bf16),
            pltpu.VMEM(queries.shape, bf16),
            pltpu.VMEM(queries.shape, bf16),
            pltpu.VMEM(queries.shape, bf16),
            pltpu.VMEM(keys.shape, bf16),
            pltpu.VMEM(values.shape, bf16),
            pltpu.VMEM((KV_HEADS, 2, WINDOW, PAIR), bf16),
            pltpu.VMEM((KV_HEADS, 2, REACH * STRETCH, PAIR), bf16),
            pltpu.VMEM((KV_HEADS, 2, STRETCH, PAIR), f32),
            pltpu.VMEM((KV_HEADS, UP_HOPS, STRETCH, PAIR), bf16),
            pltpu.VMEM((WINDOW, ROWS), f32),
            pltpu.VMEM((WINDOW, ROWS), f32),
            pltpu.VMEM((WINDOW, ROWS), bf16),
            pltpu.VMEM((WINDOW, ROWS), bf16),
            pltpu.SemaphoreType.DMA((5,)),
            pltpu.SemaphoreType.DMA((2, KV_HEADS, 2)),
            pltpu.SemaphoreType.DMA((2, KV_HEADS)),
            down, slot, slot, up,
        ],
        compiler_params=pltpu.CompilerParams(
            collective_id=0, has_side_effects=True, vmem_limit_bytes=60 * 2**20
        ),
    )(doc_blocks, queries, keys, values, grad_out)
    return pl.pallas_call(
        hand_over,
        out_shape=shapes,
        in_specs=[hbm] * 4,
        out_specs=(hbm,) * 4,
        scratch_shapes=[pltpu.VMEM(a.shape, bf16) for a in shapes]
        + [pltpu.SemaphoreType.DMA((4, PIECES))] * 2,
        compiler_params=pltpu.CompilerParams(vmem_limit_bytes=60 * 2**20),
    )(*results)


def solution(mesh):
    token = P(("dp", "ctx"), None)
    return jax.shard_map(
        local, mesh=mesh, in_specs=(token, token, token, token, P("dp")),
        out_specs=(token,) * 4, check_vma=False,
    )
```

```python
import jax
import jax.numpy as jnp
from jax import lax
from jax.experimental import pallas as pl
from jax.experimental.pallas import tpu as pltpu
from jax.sharding import PartitionSpec as P

HEADS = 32
KV_HEADS = 4
HEAD_DIM = 128
GROUPS = HEADS // KV_HEADS
STRETCH = 64
REACH = 8
WINDOW = (REACH + 1) * STRETCH
ROWS = GROUPS * STRETCH
PAIR = 2 * HEAD_DIM
MESH = pl.DeviceIdType.MESH
SCALE = HEAD_DIM ** (-0.5)
SCALE_LOG2E = SCALE * 1.4426950408889634


def dot_nt(a, b):
    return lax.dot_general(a, b, (((1,), (1,)), ((), ())), preferred_element_type=jnp.float32)


def dot_nn(a, b):
    return lax.dot_general(a, b, (((1,), (0,)), ((), ())), preferred_element_type=jnp.float32)


N, LAST = 16, 31

DOWN = (
    (0, 3, 0, 0, 1, 7, 3, 4,),
    (1, 2, 5, 1, 5, 3, 4, 5,),
    (2, 5, 6, 2, 4, 4, 5, 6,),
    (7, 4, 5, 3, 4, 5, 11, 7,),
    (4, 5, 4, 4, 8, 9, 7, 8,),
    (5, 6, 9, 5, 6, 8, 13, 9,),
    (6, 11, 13, 6, 10, 13, 14, 10,),
    (11, 10, 11, 7, 8, 9, 10, 14,),
    (8, 9, 15, 8, 9, 15, 12,),
    (9, 15, 13, 9, 15, 12,),
    (10, 15, 14, 10, 11,),
    (15, 12, 15, 11,),
    (15, 12, 15, 12,),
    (14, 15, 15, 13, 14,),
    (10, 14, 10, 15, 14, 14,),
    (11, 13, 11, 15, 15, 12, 10,),
    (11, 12, 13, 14, 15, 15, 12, 15,),
    (10, 6, 12, 10, 14, 10, 13, 14,),
    (9, 5, 6, 9, 13, 9, 10, 13,),
    (8, 9, 7, 11, 12, 8, 9, 8,),
    (7, 7, 6, 7, 11, 11, 8, 6,),
    (6, 2, 8, 6, 10, 6, 9, 10,),
    (5, 1, 2, 8, 9, 2, 4, 9,),
    (4, 0, 3, 7, 8, 1, 7, 4,),
    (3, 0, 3, 7, 7, 4, 2,),
    (3, 2, 6, 2, 0, 6,),
    (4, 5, 1, 0, 5,),
    (4, 0, 3, 0,),
    (3, 2, 3,),
    (1, 2,),
    (1,),
    (),
)
UP = (
    (2, 0, 2, 0, 4, 5, 4, 4,),
    (3, 1, 5, 1, 2, 4, 4, 5,),
    (2, 5, 6, 2, 3, 10, 5, 2,),
    (7, 7, 7, 3, 11, 8, 11, 3,),
    (4, 7, 4, 4, 5, 6, 8, 8,),
    (7, 5, 9, 5, 6, 7, 13, 5,),
    (6, 11, 10, 6, 7, 13, 14, 6,),
    (12, 11, 14, 7, 15, 9, 15, 7,),
    (13, 11, 8, 8, 12, 13, 12,),
    (9, 10, 13, 9, 12, 11,),
    (10, 13, 14, 10, 14,),
    (15, 12, 15, 11,),
    (15, 12, 15, 12,),
    (14, 15, 15, 13, 14,),
    (13, 14, 10, 13, 14, 14,),
    (12, 13, 14, 15, 15, 12, 15,),
    (15, 12, 8, 14, 15, 15, 14, 12,),
    (10, 11, 9, 10, 14, 10, 14, 9,),
    (13, 5, 6, 9, 13, 6, 8, 8,),
    (12, 9, 10, 4, 12, 8, 8, 8,),
    (11, 7, 4, 10, 11, 11, 8, 11,),
    (6, 2, 8, 9, 10, 6, 9, 10,),
    (5, 1, 1, 8, 9, 5, 4, 9,),
    (4, 0, 0, 7, 8, 4, 7, 4,),
    (4, 5, 3, 7, 5, 7, 2,),
    (2, 2, 6, 2, 5, 6,),
    (1, 5, 1, 0, 0,),
    (4, 0, 0, 0,),
    (1, 2, 3,),
    (1, 2,),
    (1,),
    (),
)
DOWN_TURNS = (8, 5, 3, 2)
UP_TURNS = (16, 10, 4)


def holder(block):
    return min(block, LAST - block)


def place(device, block):
    if block in (device, LAST - device):
        return (0, 0) if block == device else (1, 0)
    low = device - block
    return (0, low) if 0 < low <= REACH else (1, LAST - device - block)


class Slot:
    def __init__(self, device, block, level):
        self.o, self.k = place(device, block)
        self.level, self.to, self.source = level, [], None


def build(tree):
    plan = [[] for _ in range(N)]
    count = [0] * N
    for block, parents in enumerate(tree):
        top = min(block + REACH, LAST)
        readers = sorted({holder(b) for b in range(block + 1, top + 1)} - {holder(block)})
        source = dict(zip(readers, parents, strict=True))
        level = {holder(block): 0}
        while len(level) <= len(readers):
            for device in readers:
                if device not in level and source[device] in level:
                    level[device] = level[source[device]] + 1
        slots = {}
        for device in sorted(level, key=lambda device: (level[device], device)):
            slots[device] = slot = Slot(device, block, level[device])
            plan[device].append(slot)
            if slot.level:
                near = source[device]
                slot.source = (near, count[near])
                slots[near].to.append((device, count[near], slot))
                count[near] += 1
    return plan, max(count)


(DOWN_PLAN, DOWN_HOPS), (UP_PLAN, UP_HOPS) = build(DOWN), build(UP)
NEAR = [
    sorted(
        {hop[0] for slot in down + up for hop in slot.to}
        | {slot.source[0] for slot in down + up if slot.source}
    )
    for down, up in zip(DOWN_PLAN, UP_PLAN, strict=True)
]


def each_device(me, emit):
    for device in range(N):

        @pl.when(me == device)
        def _():
            emit(device)


def span(k):
    return slice((REACH - k) * STRETCH, (REACH - k + 1) * STRETCH)


def kernel(
    docs_hbm, q_hbm, k_hbm, v_hbm, do_hbm, o_hbm, dq_hbm, dk_hbm, dv_hbm,
    docs, q_buf, k_buf, v_buf, do_buf, o_buf, dq_buf, dk_buf, dv_buf, win, part, diag, coming,
    s_ref, dp_ref, p_ref, ds_ref, fetch, store, keep, gsend, grecv, rsend, rrecv,
):
    me = lax.axis_index("ctx")
    last = LAST

    fetches = [
        pltpu.make_async_copy(a, b, fetch.at[i])
        for i, (a, b) in enumerate(
            [(k_hbm, k_buf), (v_hbm, v_buf), (docs_hbm, docs), (q_hbm, q_buf), (do_hbm, do_buf)]
        )
    ]
    for copy in fetches:
        copy.start()

    barrier = pltpu.get_barrier_semaphore()

    def greet(device):
        for near in NEAR[device]:
            pl.semaphore_signal(barrier, inc=1, device_id={"ctx": near}, device_id_type=MESH)

    each_device(me, greet)
    fetches[0].wait()
    fetches[1].wait()
    for g in range(KV_HEADS):
        cols = slice(g * HEAD_DIM, (g + 1) * HEAD_DIM)
        for o in range(2):
            rows = slice(o * STRETCH, (o + 1) * STRETCH)
            win[g, o, span(0), :HEAD_DIM] = k_buf[rows, cols]
            win[g, o, span(0), HEAD_DIM:] = v_buf[rows, cols]

    @pl.loop(0, KV_HEADS)
    def _(g):
        for k in range(1, REACH + 1):

            @pl.when(me < k)
            def _():
                win[g, 0, span(k), :] = jnp.zeros((STRETCH, PAIR), jnp.bfloat16)

    each_device(me, lambda device: pl.semaphore_wait(barrier, len(NEAR[device])))

    def arrived(g, slot):
        here = win.at[g, slot.o, span(slot.k)]
        pltpu.make_async_copy(here, here, grecv.at[g, slot.o, slot.k - 1]).wait()

    def spread(level, g):
        def emit(device):
            for slot in DOWN_PLAN[device]:
                if slot.level != level or not slot.to:
                    continue
                if slot.k:
                    arrived(g, slot)
                for there, e, other in slot.to:
                    pltpu.make_async_remote_copy(
                        win.at[g, slot.o, span(slot.k)], win.at[g, other.o, span(other.k)],
                        gsend.at[g, e], grecv.at[g, other.o, other.k - 1],
                        device_id={"ctx": there}, device_id_type=MESH,
                    ).start()

        each_device(me, emit)

    def twins(device):
        base = last - 2 * device
        return [(k, k + base) for k in range(REACH + 1) if k <= device and k + base <= REACH]

    def complete(g):
        def emit(device):
            for slot in DOWN_PLAN[device]:
                if slot.k and not slot.to:
                    arrived(g, slot)
            for low, high in twins(device):
                win[g, 1, span(high), :] = win[g, 0, span(low), :]

        each_device(me, emit)

    def doc_start(block):
        end = jnp.int32(0)
        start = jnp.int32(0)
        for d in range(8):
            end = end + docs[d]
            start = jnp.where(end <= block, end, start)
        return start

    col = lax.broadcasted_iota(jnp.int32, (STRETCH, ROWS), 0)
    row_of = lax.rem(lax.broadcasted_iota(jnp.int32, (STRETCH, ROWS), 1), STRETCH)
    later = row_of < col

    def eights(x, op):
        return op(x.reshape(STRETCH // 8, 8, ROWS), axis=0)

    def head_rows(ref, o, g):
        r = pl.multiple_of(o * STRETCH, STRETCH)
        return jnp.concatenate(
            [
                ref[
                    pl.ds(r, STRETCH),
                    pl.ds(pl.multiple_of((g * GROUPS + h) * HEAD_DIM, HEAD_DIM), HEAD_DIM),
                ]
                for h in range(GROUPS)
            ],
            axis=0,
        )

    def put_heads(ref, o, g, value):
        r = pl.multiple_of(o * STRETCH, STRETCH)
        for h in range(GROUPS):
            ref[
                pl.ds(r, STRETCH),
                pl.ds(pl.multiple_of((g * GROUPS + h) * HEAD_DIM, HEAD_DIM), HEAD_DIM),
            ] = value[h * STRETCH : (h + 1) * STRETCH]

    def stores(g, o):
        rows = pl.ds(pl.multiple_of(o * STRETCH, STRETCH), STRETCH)
        width = GROUPS * HEAD_DIM
        cols = pl.ds(pl.multiple_of(g * width, width), width)
        return [
            pltpu.make_async_copy(a.at[rows, cols], b.at[rows, cols], store.at[i, g, o])
            for i, (a, b) in enumerate([(o_buf, o_hbm), (dq_buf, dq_hbm)])
        ]

    def keeps(g):
        cols = pl.ds(pl.multiple_of(g * HEAD_DIM, HEAD_DIM), HEAD_DIM)
        return [
            pltpu.make_async_copy(a.at[:, cols], b.at[:, cols], keep.at[i, g])
            for i, (a, b) in enumerate([(dk_buf, dk_hbm), (dv_buf, dv_hbm)])
        ]

    spans = [slice(kb * STRETCH, (kb + 1) * STRETCH) for kb in range(REACH + 1)]

    def products(g, o):
        q = head_rows(q_buf, o, g)
        do = head_rows(do_buf, o, g)
        s_ref[o] = dot_nt(win[g, o, :, :HEAD_DIM], q)
        dp_ref[o] = dot_nt(win[g, o, :, HEAD_DIM:], do)

    def weights(o):
        block = last - me if o else me
        start = doc_start(block)
        bias = [
            jnp.where(block - (REACH - kb) >= start, jnp.float32(0), jnp.float32(-jnp.inf))
            for kb in range(REACH + 1)
        ]
        on_diag = jnp.where(later, -jnp.inf, s_ref[o, spans[REACH], :])
        s_ref[o, spans[REACH], :] = on_diag
        top = eights(on_diag, jnp.max)
        for kb in range(REACH):
            top = jnp.maximum(top, eights(s_ref[o, spans[kb], :], jnp.max) + bias[kb])
        top = jnp.max(top, axis=0, keepdims=True) * SCALE_LOG2E
        total = jnp.zeros((8, ROWS), jnp.float32)
        inner = jnp.zeros((8, ROWS), jnp.float32)
        for kb in range(REACH + 1):
            e = jnp.exp2(s_ref[o, spans[kb], :] * SCALE_LOG2E + (bias[kb] - top))
            s_ref[o, spans[kb], :] = e
            total = total + eights(e, jnp.sum)
            inner = inner + eights(e * dp_ref[o, spans[kb], :], jnp.sum)
        inverse = 1.0 / jnp.sum(total, axis=0, keepdims=True)
        inner = jnp.sum(inner, axis=0, keepdims=True) * inverse
        for kb in range(REACH + 1):
            p = s_ref[o, spans[kb], :] * inverse
            p_ref[o, spans[kb], :] = p.astype(jnp.bfloat16)
            ds = p * (dp_ref[o, spans[kb], :] - inner)
            ds_ref[o, spans[kb], :] = ds.astype(jnp.bfloat16)

    def gradients(g, o):
        dv = dot_nn(p_ref[o], head_rows(do_buf, o, g))
        dk = SCALE * dot_nn(ds_ref[o], head_rows(q_buf, o, g))
        edge = REACH * STRETCH
        part[g, o, :edge, :HEAD_DIM] = dk[:edge].astype(jnp.bfloat16)
        part[g, o, :edge, HEAD_DIM:] = dv[:edge].astype(jnp.bfloat16)
        diag[g, o, :, :HEAD_DIM] = dk[edge:]
        diag[g, o, :, HEAD_DIM:] = dv[edge:]

    def outputs(g, o):
        vals = win[g, o, :, HEAD_DIM:]
        keys = win[g, o, :, :HEAD_DIM]
        put_heads(o_buf, o, g, dot_nn(vals.T, p_ref[o]).astype(jnp.bfloat16).T)
        put_heads(dq_buf, o, g, (SCALE * dot_nn(keys.T, ds_ref[o])).astype(jnp.bfloat16).T)

    def pair(g):
        for o in (1, 0):
            products(g, o)
        for o in (1, 0):
            weights(o)
            gradients(g, o)
            outputs(g, o)
        for copy in stores(g, 1) + stores(g, 0):
            copy.start()

    def send_home(g, device, slot):
        there, e = slot.source
        pltpu.make_async_remote_copy(
            part.at[g, slot.o, span(slot.k)], coming.at[g, e],
            rsend.at[g, slot.o, slot.k - 1], rrecv.at[g, e],
            device_id={"ctx": there}, device_id_type=MESH,
        ).start()

    def leaves(g, o):
        def emit(device):
            if o == 0:
                for low, high in twins(device):
                    twin = part[g, 1, span(high), :].astype(jnp.float32)
                    if low:
                        total = part[g, 0, span(low), :].astype(jnp.float32) + twin
                        part[g, 0, span(low), :] = total.astype(jnp.bfloat16)
                    else:
                        diag[g, 0] = diag[g, 0] + twin
            for slot in sorted(UP_PLAN[device], key=lambda slot: -slot.level):
                if slot.k and slot.o == o and not slot.to:
                    send_home(g, device, slot)

        each_device(me, emit)

    def collect(level, g):
        def emit(device):
            for slot in UP_PLAN[device]:
                if slot.level != level or not slot.to:
                    continue
                for _, e, _ in slot.to:
                    there = coming.at[g, e]
                    pltpu.make_async_copy(there, there, rrecv.at[g, e]).wait()
                if slot.k:
                    total = part[g, slot.o, span(slot.k), :].astype(jnp.float32)
                else:
                    total = diag[g, slot.o]
                for _, e, _ in slot.to:
                    total = total + coming[g, e].astype(jnp.float32)
                if slot.k:
                    part[g, slot.o, span(slot.k), :] = total.astype(jnp.bfloat16)
                    send_home(g, device, slot)
                else:
                    diag[g, slot.o] = total

        each_device(me, emit)
        if level == 0:
            cols = pl.ds(pl.multiple_of(g * HEAD_DIM, HEAD_DIM), HEAD_DIM)
            for o in range(2):
                rows = slice(o * STRETCH, (o + 1) * STRETCH)
                dk_buf[rows, cols] = diag[g, o, :, :HEAD_DIM].astype(jnp.bfloat16)
                dv_buf[rows, cols] = diag[g, o, :, HEAD_DIM:].astype(jnp.bfloat16)
            for copy in keeps(g):
                copy.start()

    tiles = 2 * KV_HEADS

    @pl.loop(-max(DOWN_TURNS), tiles + max(UP_TURNS))
    def _(turn):
        for level, ahead in enumerate(DOWN_TURNS):
            g = turn + ahead

            @pl.when((g >= 0) & (g < KV_HEADS))
            def _():
                spread(level, g)

        @pl.when(turn == 0)
        def _():
            for copy in fetches[2:]:
                copy.wait()

        @pl.when((turn >= 0) & (turn < tiles) & (lax.rem(turn, 2) == 0))
        def _():
            g = turn // 2
            complete(g)
            pair(g)
            leaves(g, 1)
            leaves(g, 0)

        for level, behind in enumerate(UP_TURNS):
            since = turn - 1 - behind

            @pl.when((since >= 0) & (lax.rem(since, 2) == 0) & (since < tiles))
            def _():
                collect(level, since // 2)

    @pl.loop(0, KV_HEADS)
    def _(g):
        def emit(device):
            for slot in DOWN_PLAN[device]:
                for _, e, _ in slot.to:
                    here = win.at[g, 0, span(0)]
                    pltpu.make_async_copy(here, here, gsend.at[g, e]).wait()
            for slot in UP_PLAN[device]:
                if slot.k:
                    here = part.at[g, slot.o, span(slot.k)]
                    pltpu.make_async_copy(here, here, rsend.at[g, slot.o, slot.k - 1]).wait()

        each_device(me, emit)
        for copy in stores(g, 0) + stores(g, 1) + keeps(g):
            copy.wait()


PIECES = 4


def hand_over(*refs):
    arrays, results, bufs, (arrive, leave) = refs[:4], refs[4:8], refs[8:12], refs[12:]
    inward, outward = [], []
    for i, (a, b, buf) in enumerate(zip(arrays, results, bufs, strict=True)):
        rows = a.shape[0] // PIECES
        for j in range(PIECES):
            piece = slice(j * rows, (j + 1) * rows)
            inward.append(pltpu.make_async_copy(a.at[piece], buf.at[piece], arrive.at[i, j]))
            outward.append(pltpu.make_async_copy(buf.at[piece], b.at[piece], leave.at[i, j]))
    for copy in inward:
        copy.start()
    for copy, after in zip(inward, outward, strict=True):
        copy.wait()
        after.start()
    for copy in outward:
        copy.wait()


def local(queries, keys, values, grad_out, doc_blocks):
    hbm = pl.BlockSpec(memory_space=pltpu.HBM)
    bf16, f32 = jnp.bfloat16, jnp.float32
    down = pltpu.SemaphoreType.DMA((KV_HEADS, DOWN_HOPS))
    up = pltpu.SemaphoreType.DMA((KV_HEADS, UP_HOPS))
    slot = pltpu.SemaphoreType.DMA((KV_HEADS, 2, REACH))
    shapes = (
        jax.ShapeDtypeStruct(queries.shape, bf16),
        jax.ShapeDtypeStruct(queries.shape, bf16),
        jax.ShapeDtypeStruct(keys.shape, bf16),
        jax.ShapeDtypeStruct(values.shape, bf16),
    )
    results = pl.pallas_call(
        kernel,
        out_shape=shapes,
        in_specs=[hbm] * 5,
        out_specs=(hbm,) * 4,
        scratch_shapes=[
            pltpu.SMEM(doc_blocks.shape, jnp.int32),
            pltpu.VMEM(queries.shape, bf16),
            pltpu.VMEM(keys.shape, bf16),
            pltpu.VMEM(values.shape, bf16),
            pltpu.VMEM(queries.shape, bf16),
            pltpu.VMEM(queries.shape, bf16),
            pltpu.VMEM(queries.shape, bf16),
            pltpu.VMEM(keys.shape, bf16),
            pltpu.VMEM(values.shape, bf16),
            pltpu.VMEM((KV_HEADS, 2, WINDOW, PAIR), bf16),
            pltpu.VMEM((KV_HEADS, 2, REACH * STRETCH, PAIR), bf16),
            pltpu.VMEM((KV_HEADS, 2, STRETCH, PAIR), f32),
            pltpu.VMEM((KV_HEADS, UP_HOPS, STRETCH, PAIR), bf16),
            pltpu.VMEM((2, WINDOW, ROWS), f32),
            pltpu.VMEM((2, WINDOW, ROWS), f32),
            pltpu.VMEM((2, WINDOW, ROWS), bf16),
            pltpu.VMEM((2, WINDOW, ROWS), bf16),
            pltpu.SemaphoreType.DMA((5,)),
            pltpu.SemaphoreType.DMA((2, KV_HEADS, 2)),
            pltpu.SemaphoreType.DMA((2, KV_HEADS)),
            down, slot, slot, up,
        ],
        compiler_params=pltpu.CompilerParams(
            collective_id=0, has_side_effects=True, vmem_limit_bytes=60 * 2**20
        ),
    )(doc_blocks, queries, keys, values, grad_out)
    return pl.pallas_call(
        hand_over,
        out_shape=shapes,
        in_specs=[hbm] * 4,
        out_specs=(hbm,) * 4,
        scratch_shapes=[pltpu.VMEM(a.shape, bf16) for a in shapes]
        + [pltpu.SemaphoreType.DMA((4, PIECES))] * 2,
        compiler_params=pltpu.CompilerParams(vmem_limit_bytes=60 * 2**20),
    )(*results)


def solution(mesh):
    token = P(("dp", "ctx"), None)
    return jax.shard_map(
        local, mesh=mesh, in_specs=(token, token, token, token, P("dp")),
        out_specs=(token,) * 4, check_vma=False,
    )
```

```python
import jax
import jax.numpy as jnp
from jax import lax
from jax.experimental import pallas as pl
from jax.experimental.pallas import tpu as pltpu
from jax.sharding import PartitionSpec as P

HEADS = 32
KV_HEADS = 4
HEAD_DIM = 128
GROUPS = HEADS // KV_HEADS
STRETCH = 64
REACH = 8
WINDOW = (REACH + 1) * STRETCH
ROWS = GROUPS * STRETCH
PAIR = 2 * HEAD_DIM
MESH = pl.DeviceIdType.MESH
SCALE = HEAD_DIM ** (-0.5)
SCALE_LOG2E = SCALE * 1.4426950408889634


def dot_nt(a, b):
    return lax.dot_general(a, b, (((1,), (1,)), ((), ())), preferred_element_type=jnp.float32)


def dot_nn(a, b):
    return lax.dot_general(a, b, (((1,), (0,)), ((), ())), preferred_element_type=jnp.float32)


N, LAST = 16, 31

DOWN = (
    (0, 3, 0, 0, 1, 7, 3, 4,),
    (1, 2, 5, 1, 5, 3, 4, 5,),
    (2, 5, 6, 2, 4, 4, 5, 6,),
    (7, 4, 5, 3, 4, 5, 11, 7,),
    (4, 5, 4, 4, 8, 9, 7, 8,),
    (5, 6, 9, 5, 6, 8, 13, 9,),
    (6, 11, 13, 6, 10, 13, 14, 10,),
    (11, 10, 11, 7, 8, 9, 10, 14,),
    (8, 9, 15, 8, 9, 15, 12,),
    (9, 15, 13, 9, 15, 12,),
    (10, 15, 14, 10, 11,),
    (15, 12, 15, 11,),
    (15, 12, 15, 12,),
    (14, 15, 15, 13, 14,),
    (10, 14, 10, 15, 14, 14,),
    (11, 13, 11, 15, 15, 12, 10,),
    (11, 12, 13, 14, 15, 15, 12, 15,),
    (10, 6, 12, 10, 14, 10, 13, 14,),
    (9, 5, 6, 9, 13, 9, 10, 13,),
    (8, 9, 7, 11, 12, 8, 9, 8,),
    (7, 7, 6, 7, 11, 11, 8, 6,),
    (6, 2, 8, 6, 10, 6, 9, 10,),
    (5, 1, 2, 8, 9, 2, 4, 9,),
    (4, 0, 3, 7, 8, 1, 7, 4,),
    (3, 0, 3, 7, 7, 4, 2,),
    (3, 2, 6, 2, 0, 6,),
    (4, 5, 1, 0, 5,),
    (4, 0, 3, 0,),
    (3, 2, 3,),
    (1, 2,),
    (1,),
    (),
)
UP = (
    (2, 0, 2, 0, 4, 5, 4, 4,),
    (3, 1, 5, 1, 2, 4, 4, 5,),
    (2, 5, 6, 2, 3, 10, 5, 2,),
    (7, 7, 7, 3, 11, 8, 11, 3,),
    (4, 7, 4, 4, 5, 6, 8, 8,),
    (7, 5, 9, 5, 6, 7, 13, 5,),
    (6, 11, 10, 6, 7, 13, 14, 6,),
    (12, 11, 14, 7, 15, 9, 15, 7,),
    (13, 11, 8, 8, 12, 13, 12,),
    (9, 10, 13, 9, 12, 11,),
    (10, 13, 14, 10, 14,),
    (15, 12, 15, 11,),
    (15, 12, 15, 12,),
    (14, 15, 15, 13, 14,),
    (13, 14, 10, 13, 14, 14,),
    (12, 13, 14, 15, 15, 12, 15,),
    (15, 12, 8, 14, 15, 15, 14, 12,),
    (10, 11, 9, 10, 14, 10, 14, 9,),
    (13, 5, 6, 9, 13, 6, 8, 8,),
    (12, 9, 10, 4, 12, 8, 8, 8,),
    (11, 7, 4, 10, 11, 11, 8, 11,),
    (6, 2, 8, 9, 10, 6, 9, 10,),
    (5, 1, 1, 8, 9, 5, 4, 9,),
    (4, 0, 0, 7, 8, 4, 7, 4,),
    (4, 5, 3, 7, 5, 7, 2,),
    (2, 2, 6, 2, 5, 6,),
    (1, 5, 1, 0, 0,),
    (4, 0, 0, 0,),
    (1, 2, 3,),
    (1, 2,),
    (1,),
    (),
)
DOWN_TURNS = (8, 5, 3, 2)
UP_TURNS = (16, 10, 4)


def holder(block):
    return min(block, LAST - block)


def place(device, block):
    if block in (device, LAST - device):
        return (0, 0) if block == device else (1, 0)
    low = device - block
    return (0, low) if 0 < low <= REACH else (1, LAST - device - block)


class Slot:
    def __init__(self, device, block, level):
        self.o, self.k = place(device, block)
        self.level, self.to, self.source = level, [], None


def build(tree):
    plan = [[] for _ in range(N)]
    count = [0] * N
    for block, parents in enumerate(tree):
        top = min(block + REACH, LAST)
        readers = sorted({holder(b) for b in range(block + 1, top + 1)} - {holder(block)})
        source = dict(zip(readers, parents, strict=True))
        level = {holder(block): 0}
        while len(level) <= len(readers):
            for device in readers:
                if device not in level and source[device] in level:
                    level[device] = level[source[device]] + 1
        slots = {}
        for device in sorted(level, key=lambda device: (level[device], device)):
            slots[device] = slot = Slot(device, block, level[device])
            plan[device].append(slot)
            if slot.level:
                near = source[device]
                slot.source = (near, count[near])
                slots[near].to.append((device, count[near], slot))
                count[near] += 1
    return plan, max(count)


(DOWN_PLAN, DOWN_HOPS), (UP_PLAN, UP_HOPS) = build(DOWN), build(UP)
NEAR = [
    sorted(
        {hop[0] for slot in down + up for hop in slot.to}
        | {slot.source[0] for slot in down + up if slot.source}
    )
    for down, up in zip(DOWN_PLAN, UP_PLAN, strict=True)
]


def each_device(me, emit):
    def halve(low, high):
        if high - low == 1:
            emit(low)
            return
        middle = (low + high) // 2

        @pl.when(me < middle)
        def _():
            halve(low, middle)

        @pl.when(me >= middle)
        def _():
            halve(middle, high)

    halve(0, N)


def span(k):
    return slice((REACH - k) * STRETCH, (REACH - k + 1) * STRETCH)


def kernel(
    docs_hbm, q_hbm, k_hbm, v_hbm, do_hbm, o_hbm, dq_hbm, dk_hbm, dv_hbm,
    docs, q_buf, k_buf, v_buf, do_buf, o_buf, dq_buf, dk_buf, dv_buf, win, part, diag, coming,
    s_ref, dp_ref, p_ref, ds_ref, fetch, store, keep, gsend, grecv, rsend, rrecv,
):
    me = lax.axis_index("ctx")
    last = LAST

    barrier = pltpu.get_barrier_semaphore()

    def greet(device):
        for near in NEAR[device]:
            pl.semaphore_signal(barrier, inc=1, device_id={"ctx": near}, device_id_type=MESH)

    each_device(me, greet)
    fetches = [
        pltpu.make_async_copy(a, b, fetch.at[i])
        for i, (a, b) in enumerate(
            [(k_hbm, k_buf), (v_hbm, v_buf), (docs_hbm, docs), (q_hbm, q_buf), (do_hbm, do_buf)]
        )
    ]
    for copy in fetches:
        copy.start()

    fetches[0].wait()
    fetches[1].wait()
    for g in range(KV_HEADS):
        cols = slice(g * HEAD_DIM, (g + 1) * HEAD_DIM)
        for o in range(2):
            rows = slice(o * STRETCH, (o + 1) * STRETCH)
            win[g, o, span(0), :HEAD_DIM] = k_buf[rows, cols]
            win[g, o, span(0), HEAD_DIM:] = v_buf[rows, cols]

    @pl.loop(0, KV_HEADS)
    def _(g):
        for k in range(1, REACH + 1):

            @pl.when(me < k)
            def _():
                win[g, 0, span(k), :] = jnp.zeros((STRETCH, PAIR), jnp.bfloat16)

    each_device(me, lambda device: pl.semaphore_wait(barrier, len(NEAR[device])))

    def arrived(g, slot):
        here = win.at[g, slot.o, span(slot.k)]
        pltpu.make_async_copy(here, here, grecv.at[g, slot.o, slot.k - 1]).wait()

    def spread(level, g):
        def emit(device):
            for slot in DOWN_PLAN[device]:
                if slot.level != level or not slot.to:
                    continue
                if slot.k:
                    arrived(g, slot)
                for there, e, other in slot.to:
                    pltpu.make_async_remote_copy(
                        win.at[g, slot.o, span(slot.k)], win.at[g, other.o, span(other.k)],
                        gsend.at[g, e], grecv.at[g, other.o, other.k - 1],
                        device_id={"ctx": there}, device_id_type=MESH,
                    ).start()

        each_device(me, emit)

    def twins(device):
        base = last - 2 * device
        return [(k, k + base) for k in range(REACH + 1) if k <= device and k + base <= REACH]

    def complete(g):
        def emit(device):
            for slot in DOWN_PLAN[device]:
                if slot.k and not slot.to:
                    arrived(g, slot)
            for low, high in twins(device):
                win[g, 1, span(high), :] = win[g, 0, span(low), :]

        each_device(me, emit)

    def doc_start(block):
        end = jnp.int32(0)
        start = jnp.int32(0)
        for d in range(8):
            end = end + docs[d]
            start = jnp.where(end <= block, end, start)
        return start

    col = lax.broadcasted_iota(jnp.int32, (STRETCH, ROWS), 0)
    row_of = lax.rem(lax.broadcasted_iota(jnp.int32, (STRETCH, ROWS), 1), STRETCH)
    later = row_of < col

    def eights(x, op):
        return op(x.reshape(STRETCH // 8, 8, ROWS), axis=0)

    def head_rows(ref, o, g):
        r = pl.multiple_of(o * STRETCH, STRETCH)
        return jnp.concatenate(
            [
                ref[
                    pl.ds(r, STRETCH),
                    pl.ds(pl.multiple_of((g * GROUPS + h) * HEAD_DIM, HEAD_DIM), HEAD_DIM),
                ]
                for h in range(GROUPS)
            ],
            axis=0,
        )

    def put_heads(ref, o, g, value):
        r = pl.multiple_of(o * STRETCH, STRETCH)
        for h in range(GROUPS):
            ref[
                pl.ds(r, STRETCH),
                pl.ds(pl.multiple_of((g * GROUPS + h) * HEAD_DIM, HEAD_DIM), HEAD_DIM),
            ] = value[h * STRETCH : (h + 1) * STRETCH]

    def stores(g, o):
        rows = pl.ds(pl.multiple_of(o * STRETCH, STRETCH), STRETCH)
        width = GROUPS * HEAD_DIM
        cols = pl.ds(pl.multiple_of(g * width, width), width)
        return [
            pltpu.make_async_copy(a.at[rows, cols], b.at[rows, cols], store.at[i, g, o])
            for i, (a, b) in enumerate([(o_buf, o_hbm), (dq_buf, dq_hbm)])
        ]

    def keeps(g):
        cols = pl.ds(pl.multiple_of(g * HEAD_DIM, HEAD_DIM), HEAD_DIM)
        return [
            pltpu.make_async_copy(a.at[:, cols], b.at[:, cols], keep.at[i, g])
            for i, (a, b) in enumerate([(dk_buf, dk_hbm), (dv_buf, dv_hbm)])
        ]

    spans = [slice(kb * STRETCH, (kb + 1) * STRETCH) for kb in range(REACH + 1)]

    def products(g, o):
        q = head_rows(q_buf, o, g)
        do = head_rows(do_buf, o, g)
        s_ref[o] = dot_nt(win[g, o, :, :HEAD_DIM], q)
        dp_ref[o] = dot_nt(win[g, o, :, HEAD_DIM:], do)

    def weights(o):
        block = last - me if o else me
        start = doc_start(block)
        bias = [
            jnp.where(block - (REACH - kb) >= start, jnp.float32(0), jnp.float32(-jnp.inf))
            for kb in range(REACH + 1)
        ]
        on_diag = jnp.where(later, -jnp.inf, s_ref[o, spans[REACH], :])
        s_ref[o, spans[REACH], :] = on_diag
        top = eights(on_diag, jnp.max)
        for kb in range(REACH):
            top = jnp.maximum(top, eights(s_ref[o, spans[kb], :], jnp.max) + bias[kb])
        top = jnp.max(top, axis=0, keepdims=True) * SCALE_LOG2E
        total = jnp.zeros((8, ROWS), jnp.float32)
        inner = jnp.zeros((8, ROWS), jnp.float32)
        for kb in range(REACH + 1):
            e = jnp.exp2(s_ref[o, spans[kb], :] * SCALE_LOG2E + (bias[kb] - top))
            s_ref[o, spans[kb], :] = e
            total = total + eights(e, jnp.sum)
            inner = inner + eights(e * dp_ref[o, spans[kb], :], jnp.sum)
        inverse = 1.0 / jnp.sum(total, axis=0, keepdims=True)
        inner = jnp.sum(inner, axis=0, keepdims=True) * inverse
        for kb in range(REACH + 1):
            p = s_ref[o, spans[kb], :] * inverse
            p_ref[o, spans[kb], :] = p.astype(jnp.bfloat16)
            ds = p * (dp_ref[o, spans[kb], :] - inner)
            ds_ref[o, spans[kb], :] = ds.astype(jnp.bfloat16)

    def gradients(g, o):
        dv = dot_nn(p_ref[o], head_rows(do_buf, o, g))
        dk = SCALE * dot_nn(ds_ref[o], head_rows(q_buf, o, g))
        edge = REACH * STRETCH
        part[g, o, :edge, :HEAD_DIM] = dk[:edge].astype(jnp.bfloat16)
        part[g, o, :edge, HEAD_DIM:] = dv[:edge].astype(jnp.bfloat16)
        diag[g, o, :, :HEAD_DIM] = dk[edge:]
        diag[g, o, :, HEAD_DIM:] = dv[edge:]

    def outputs(g, o):
        vals = win[g, o, :, HEAD_DIM:]
        keys = win[g, o, :, :HEAD_DIM]
        put_heads(o_buf, o, g, dot_nn(vals.T, p_ref[o]).astype(jnp.bfloat16).T)
        put_heads(dq_buf, o, g, (SCALE * dot_nn(keys.T, ds_ref[o])).astype(jnp.bfloat16).T)

    def pair(g):
        for o in (1, 0):
            products(g, o)
        for o in (1, 0):
            weights(o)
            gradients(g, o)
            outputs(g, o)
        for copy in stores(g, 1) + stores(g, 0):
            copy.start()

    def send_home(g, device, slot):
        there, e = slot.source
        pltpu.make_async_remote_copy(
            part.at[g, slot.o, span(slot.k)], coming.at[g, e],
            rsend.at[g, slot.o, slot.k - 1], rrecv.at[g, e],
            device_id={"ctx": there}, device_id_type=MESH,
        ).start()

    def leaves(g, o):
        def emit(device):
            if o == 0:
                for low, high in twins(device):
                    twin = part[g, 1, span(high), :].astype(jnp.float32)
                    if low:
                        total = part[g, 0, span(low), :].astype(jnp.float32) + twin
                        part[g, 0, span(low), :] = total.astype(jnp.bfloat16)
                    else:
                        diag[g, 0] = diag[g, 0] + twin
            for slot in sorted(UP_PLAN[device], key=lambda slot: -slot.level):
                if slot.k and slot.o == o and not slot.to:
                    send_home(g, device, slot)

        each_device(me, emit)

    def collect(level, g):
        def emit(device):
            for slot in UP_PLAN[device]:
                if slot.level != level or not slot.to:
                    continue
                for _, e, _ in slot.to:
                    there = coming.at[g, e]
                    pltpu.make_async_copy(there, there, rrecv.at[g, e]).wait()
                if slot.k:
                    total = part[g, slot.o, span(slot.k), :].astype(jnp.float32)
                else:
                    total = diag[g, slot.o]
                for _, e, _ in slot.to:
                    total = total + coming[g, e].astype(jnp.float32)
                if slot.k:
                    part[g, slot.o, span(slot.k), :] = total.astype(jnp.bfloat16)
                    send_home(g, device, slot)
                else:
                    diag[g, slot.o] = total

        each_device(me, emit)
        if level == 0:
            cols = pl.ds(pl.multiple_of(g * HEAD_DIM, HEAD_DIM), HEAD_DIM)
            for o in range(2):
                rows = slice(o * STRETCH, (o + 1) * STRETCH)
                dk_buf[rows, cols] = diag[g, o, :, :HEAD_DIM].astype(jnp.bfloat16)
                dv_buf[rows, cols] = diag[g, o, :, HEAD_DIM:].astype(jnp.bfloat16)
            for copy in keeps(g):
                copy.start()

    tiles = 2 * KV_HEADS

    @pl.loop(-max(DOWN_TURNS), tiles + max(UP_TURNS))
    def _(turn):
        for level, ahead in enumerate(DOWN_TURNS):
            g = turn + ahead

            @pl.when((g >= 0) & (g < KV_HEADS))
            def _():
                spread(level, g)

        @pl.when(turn == 0)
        def _():
            for copy in fetches[2:]:
                copy.wait()

        @pl.when((turn >= 0) & (turn < tiles) & (lax.rem(turn, 2) == 0))
        def _():
            g = turn // 2
            complete(g)
            pair(g)
            leaves(g, 1)
            leaves(g, 0)

        for level, behind in enumerate(UP_TURNS):
            since = turn - 1 - behind

            @pl.when((since >= 0) & (lax.rem(since, 2) == 0) & (since < tiles))
            def _():
                collect(level, since // 2)

    @pl.loop(0, KV_HEADS)
    def _(g):
        def emit(device):
            for slot in DOWN_PLAN[device]:
                for _, e, _ in slot.to:
                    here = win.at[g, 0, span(0)]
                    pltpu.make_async_copy(here, here, gsend.at[g, e]).wait()
            for slot in UP_PLAN[device]:
                if slot.k:
                    here = part.at[g, slot.o, span(slot.k)]
                    pltpu.make_async_copy(here, here, rsend.at[g, slot.o, slot.k - 1]).wait()

        each_device(me, emit)
        for copy in stores(g, 0) + stores(g, 1) + keeps(g):
            copy.wait()


PIECES = 4


def hand_over(*refs):
    arrays, results, bufs, (arrive, leave) = refs[:4], refs[4:8], refs[8:12], refs[12:]
    inward, outward = [], []
    for i, (a, b, buf) in enumerate(zip(arrays, results, bufs, strict=True)):
        rows = a.shape[0] // PIECES
        for j in range(PIECES):
            piece = slice(j * rows, (j + 1) * rows)
            inward.append(pltpu.make_async_copy(a.at[piece], buf.at[piece], arrive.at[i, j]))
            outward.append(pltpu.make_async_copy(buf.at[piece], b.at[piece], leave.at[i, j]))
    for copy in inward:
        copy.start()
    for copy, after in zip(inward, outward, strict=True):
        copy.wait()
        after.start()
    for copy in outward:
        copy.wait()


def local(queries, keys, values, grad_out, doc_blocks):
    hbm = pl.BlockSpec(memory_space=pltpu.HBM)
    bf16, f32 = jnp.bfloat16, jnp.float32
    down = pltpu.SemaphoreType.DMA((KV_HEADS, DOWN_HOPS))
    up = pltpu.SemaphoreType.DMA((KV_HEADS, UP_HOPS))
    slot = pltpu.SemaphoreType.DMA((KV_HEADS, 2, REACH))
    shapes = (
        jax.ShapeDtypeStruct(queries.shape, bf16),
        jax.ShapeDtypeStruct(queries.shape, bf16),
        jax.ShapeDtypeStruct(keys.shape, bf16),
        jax.ShapeDtypeStruct(values.shape, bf16),
    )
    results = pl.pallas_call(
        kernel,
        out_shape=shapes,
        in_specs=[hbm] * 5,
        out_specs=(hbm,) * 4,
        scratch_shapes=[
            pltpu.SMEM(doc_blocks.shape, jnp.int32),
            pltpu.VMEM(queries.shape, bf16),
            pltpu.VMEM(keys.shape, bf16),
            pltpu.VMEM(values.shape, bf16),
            pltpu.VMEM(queries.shape, bf16),
            pltpu.VMEM(queries.shape, bf16),
            pltpu.VMEM(queries.shape, bf16),
            pltpu.VMEM(keys.shape, bf16),
            pltpu.VMEM(values.shape, bf16),
            pltpu.VMEM((KV_HEADS, 2, WINDOW, PAIR), bf16),
            pltpu.VMEM((KV_HEADS, 2, REACH * STRETCH, PAIR), bf16),
            pltpu.VMEM((KV_HEADS, 2, STRETCH, PAIR), f32),
            pltpu.VMEM((KV_HEADS, UP_HOPS, STRETCH, PAIR), bf16),
            pltpu.VMEM((2, WINDOW, ROWS), f32),
            pltpu.VMEM((2, WINDOW, ROWS), f32),
            pltpu.VMEM((2, WINDOW, ROWS), bf16),
            pltpu.VMEM((2, WINDOW, ROWS), bf16),
            pltpu.SemaphoreType.DMA((5,)),
            pltpu.SemaphoreType.DMA((2, KV_HEADS, 2)),
            pltpu.SemaphoreType.DMA((2, KV_HEADS)),
            down, slot, slot, up,
        ],
        compiler_params=pltpu.CompilerParams(
            collective_id=0, has_side_effects=True, vmem_limit_bytes=60 * 2**20
        ),
    )(doc_blocks, queries, keys, values, grad_out)
    return pl.pallas_call(
        hand_over,
        out_shape=shapes,
        in_specs=[hbm] * 4,
        out_specs=(hbm,) * 4,
        scratch_shapes=[pltpu.VMEM(a.shape, bf16) for a in shapes]
        + [pltpu.SemaphoreType.DMA((4, PIECES))] * 2,
        compiler_params=pltpu.CompilerParams(vmem_limit_bytes=60 * 2**20),
    )(*results)


def solution(mesh):
    token = P(("dp", "ctx"), None)
    return jax.shard_map(
        local, mesh=mesh, in_specs=(token, token, token, token, P("dp")),
        out_specs=(token,) * 4, check_vma=False,
    )
```
